512 devices in a mesh: span: 16 (over z, core), grp: 32 (over y, x).
Axes of the slice: x: 4, y: 8, z: 8, core: 2. Of those that a mesh axis runs over, the one named last changes fastest.
Arguments:
- displacement: float32 [16, 5, 32768], P('span', None, 'grp'), may hold values from -3 to 3
- velocity: float32 [16, 5, 32768], P('span', None, 'grp'), may hold values from -3 to 3
- nodal_load: float32 [16, 5, 32768], P('span', None, 'grp'), may hold values from -6 to 6
- nodal_mass: float32 [16, 32768], P('span', 'grp'), may hold values from 1 to 4
- plastic_strain: float32 [16, 512, 3, 5, 128], P('span', 'grp'), may hold values from -0.3 to 0.3
- hardening: float32 [16, 512, 5, 128], P('span', 'grp'), may hold values from 0 to 0.2
- ply_modulus: float32 [16, 512, 5, 128], P('span', 'grp'), may hold values from 0.5 to 2
- inverse_size: float32 [16, 512, 128], P('span', 'grp'), may hold values from 0.5 to 2
- cost_map: int32 [16, 512], P('span'), may hold values from 1 to 4
- migration_plan: int32 [16, 512, 1], P('span'), may hold values from 0 to 31; in each aligned block of 16 rows (0 to 15, 16 to 31, ..., all dimensions but the last counted through in order) no two rows name the same one
- block_nodes: int32 [16, 512, 256], P('span'), may hold values from 0 to 32959, as said below
- corner_slot: int32 [16, 512, 4, 128], P('span'), may hold values from 0 to 255
Outputs:
- displacement_out: float32 [16, 5, 32768], P('span', None, 'grp')
- velocity_out: float32 [16, 5, 32768], P('span', None, 'grp')
- resident_plastic: float32 [16, 1024, 3, 5, 128], P('span', 'grp')
- resident_hardening: float32 [16, 1024, 5, 128], P('span', 'grp')
The draws below stay inside these ranges and needn't reach their ends.
Inputs may be any that keep to these rules, and one draw needn't show every extreme that they name: `migration_plan`: of the 16 blocks that start on one device (aligned blocks of 16 entries), no more than 1 name the same device. `cost_map`: newton turns of a block. `block_nodes`: block b of a span group (0 to 511) lists 256 distinct nodes from b * (64) on.
All inputs are finite; a program needn't handle non-finite values.
Results may differ from the reference program's by a relative error of at most 0.0003.
Values sent between devices are 32-bit elements; how exact they have to be, the bound alone decides.
No kernel may reach another device: no remote copies, remote signals or barrier semaphores. Data moves between devices by JAX's collectives and lax.ppermute only.
A program may use at most 64 MiB of HBM per device.

```python
import math
import jax
import jax.numpy as jnp
import numpy as np
from jax import lax

NOWN = 1024
BLK = 16
EL = 128
PTS = 5
WINDOW = 256
NEWTON = 4
STEPS = 4
CAP = 1
NGN = 32768
N_SPAN = 16
N_GRP = 32


def draw_block_nodes(key, part):
    count = N_SPAN * N_GRP * BLK
    keys = jax.random.split(jax.random.fold_in(key, 7), count)

    def one_list(subkey):
        return jax.random.permutation(subkey, WINDOW)
    lists = jax.vmap(one_list)(keys).astype(jnp.int32).reshape(N_SPAN, N_GRP * BLK, WINDOW)
    base = jnp.arange(N_GRP * BLK, dtype=jnp.int32) * (NOWN // BLK)
    return (base[None, :, None] + lists).astype(jnp.int32)


def with_ends(drawn, key, low, high):
    shape = drawn.shape
    spot = [jax.random.randint(jax.random.fold_in(key, axis), (), 0, shape[axis]) for axis in range(len(shape))]
    drawn = drawn.at[tuple(spot)].set(low)
    longest = shape.index(max(shape))
    spot[longest] = (spot[longest] + 1) % shape[longest]
    return drawn.at[tuple(spot)].set(high)


def block_scale(rng, dims, cuts, least, high):
    level = 1.0
    for axis_at, blocks in cuts:
        steps = jax.random.uniform(jax.random.fold_in(jax.random.fold_in(rng, 6), axis_at), (blocks,), jnp.float32, least / len(cuts), high / len(cuts))
        level = level * jnp.repeat(jnp.exp(steps), dims[axis_at] // blocks).reshape((-1,) + (1,) * (len(dims) - 1 - axis_at))
    return level


def shared_out(own_key, own, number, rows, count, top, reach, lean):
    ranking = jax.random.permutation(own_key, count)
    crowded, ordinary = load_shares(count, rows * top, reach, lean, True), load_shares(count, rows * top, reach, lean, False)
    places = jnp.arange(count)

    def named(sizes, offset_by):
        used = int((sizes > 0).sum())
        fixed = max(1, used // 4)
        passed = fixed + (places - fixed + offset_by * (used - fixed)) % max(1, count - fixed)
        return jnp.zeros((count,), jnp.int32).at[ranking[jnp.where(places < fixed, places, passed)]].set(jnp.asarray(sizes, jnp.int32))

    sizes = jnp.where(number % 4 == 0, named(crowded, number // 4), named(ordinary, number - number // 4 - 1))
    mixed = jax.random.permutation(jax.random.fold_in(own, 3), count)
    donor, sink = mixed[0:count // 2 * 2:2], mixed[1:count // 2 * 2:2]
    margin = jnp.minimum(sizes[donor] - 1, reach - sizes[sink]) // 2
    margin = jnp.where((donor == ranking[0]) | (sink == ranking[0]) | (sizes[sink] == 0), 0, jnp.maximum(margin, 0))
    passed = jax.random.randint(jax.random.fold_in(own, 4), (count // 2,), 0, 1 << 20) % (margin + 1)
    sizes = sizes.at[donor].add(-passed).at[sink].add(passed)
    members = jnp.searchsorted(jnp.cumsum(sizes), jnp.arange(rows * top), side="right").astype(jnp.int32)
    table = members.reshape(top, rows).T
    table = table[jax.random.permutation(jax.random.fold_in(own, 1), rows)]
    offset_by = jax.random.randint(jax.random.fold_in(own, 2), (rows, 1), 0, top)
    return jnp.take_along_axis(table, (jnp.arange(top)[None, :] + offset_by) % top, axis=1)


def load_shares(number_of, total, limit, slope, full):
    weights = [(1 << 20) // math.isqrt(grade ** slope) + 1 for grade in range(1, number_of + 1)]
    largest = limit if full else min(limit, max(-(-total // number_of), total * weights[0] // sum(weights)))
    least = 1 if total - largest >= number_of - 1 else 0
    holding, surplus = [largest] + [least] * (number_of - 1), total - largest - least * (number_of - 1)
    while surplus > 0:
        free = [i for i in range(1, number_of) if holding[i] < largest] or [i for i in range(1, number_of) if holding[i] < limit]
        pool, remaining = sum([weights[i] for i in free]), surplus
        for i in free:
            extra = min(limit - holding[i], max(1, remaining * weights[i] // pool), surplus)
            holding[i] = holding[i] + extra
            surplus = surplus - extra
    return np.array(holding)


def centred(rng, dims, width, most, shards=(), held_as=jnp.bfloat16):
    values = jax.random.normal(rng, dims, jnp.float32) * width
    if len(shards) > 0:
        values = block_scale(rng, dims, shards, -0.22, 0.18) * values
    return jnp.clip(values, min=-most, max=most).astype(held_as)


def setup_inputs(seed: int = 0) -> dict:
    seeds = jax.random.split(jax.random.key(seed), 13)
    displacement = centred(seeds[0], (N_SPAN, 5, NGN), 0.5, 3.0, ((0, 16), (2, 32)), jnp.float32)
    velocity = centred(seeds[1], (N_SPAN, 5, NGN), 0.5, 3.0, ((0, 16), (2, 32)), jnp.float32)
    nodal_load = centred(seeds[2], (N_SPAN, 5, NGN), 1.0, 6.0, ((0, 16), (2, 32)), jnp.float32)
    nodal_mass = jnp.clip(jnp.exp(math.log(4.0) - 1.3862944 * jax.random.uniform(seeds[3], (N_SPAN, NGN), jnp.float32) ** block_scale(seeds[3], (N_SPAN, NGN), ((0, 16), (1, 32)), -0.2, 0.2)), 1.0, 4.0)
    plastic_strain = centred(seeds[4], (N_SPAN, N_GRP * BLK, 3, PTS, EL), 0.05, 0.3, ((0, 16), (1, 32)), jnp.float32)
    hardening = jnp.clip(0.2 * jax.random.uniform(seeds[5], (N_SPAN, N_GRP * BLK, PTS, EL), jnp.float32) ** block_scale(seeds[5], (N_SPAN, N_GRP * BLK, PTS, EL), ((0, 16), (1, 32)), -0.2, 0.2), 0.0, 0.2)
    ply_modulus = jnp.clip(jnp.exp(math.log(2.0) - 1.3862944 * jax.random.uniform(seeds[6], (N_SPAN, N_GRP * BLK, PTS, EL), jnp.float32) ** block_scale(seeds[6], (N_SPAN, N_GRP * BLK, PTS, EL), ((0, 16), (1, 32)), -0.2, 0.2)), 0.5, 2.0)
    inverse_size = jnp.clip(jnp.exp(math.log(2.0) - 1.3862944 * jax.random.uniform(seeds[7], (N_SPAN, N_GRP * BLK, EL), jnp.float32) ** block_scale(seeds[7], (N_SPAN, N_GRP * BLK, EL), ((0, 16), (1, 32)), -0.2, 0.2)), 0.5, 2.0)
    cost_map = with_ends(jax.random.randint(seeds[8], (N_SPAN, N_GRP * BLK), 1, NEWTON + 1), jax.random.fold_in(seeds[8], 1), 1, NEWTON).astype(jnp.int32)
    migration_plan_keys = jax.random.split(jax.random.fold_in(seeds[9], 1), N_SPAN * (N_GRP * BLK) // BLK)
    migration_plan_turns = jax.random.permutation(jax.random.fold_in(seeds[9], 3), N_SPAN * (N_GRP * BLK) // BLK)
    migration_plan = jax.vmap(lambda own, number: shared_out(jax.random.fold_in(seeds[9], 2), own, number, BLK, N_GRP, 1, CAP, 1))(migration_plan_keys, migration_plan_turns).reshape((N_SPAN, N_GRP * BLK, 1))
    block_nodes = draw_block_nodes(jax.random.fold_in(seeds[12], 71), 0)
    corner_slot = with_ends(jax.random.randint(seeds[11], (N_SPAN, N_GRP * BLK, 4, EL), 0, WINDOW), jax.random.fold_in(seeds[11], 1), 0, WINDOW - 1).astype(jnp.int32)
    return dict(displacement=displacement, velocity=velocity, nodal_load=nodal_load, nodal_mass=nodal_mass, plastic_strain=plastic_strain, hardening=hardening, ply_modulus=ply_modulus, inverse_size=inverse_size, cost_map=cost_map, migration_plan=migration_plan, block_nodes=block_nodes, corner_slot=corner_slot)


POISSON = 0.3
YIELD = 0.1
SATURATE = 0.1
RATE = 20.0
STEP_TIME = 0.25

def element_update(corner_disp, inverse_size, modulus, plastic, harden, costs):
    corner_a = corner_disp[:, :, 0]
    corner_b = corner_disp[:, :, 1]
    corner_c = corner_disp[:, :, 2]
    corner_d = corner_disp[:, :, 3]
    inverse = inverse_size[:, None, :]
    deriv_x = 0.5 * inverse * (corner_b + corner_c - corner_a - corner_d)
    deriv_y = 0.5 * inverse * (corner_c + corner_d - corner_a - corner_b)
    centre = 0.25 * (corner_a + corner_b + corner_c + corner_d)
    membrane = jnp.stack([deriv_x[:, 0], deriv_y[:, 1], deriv_y[:, 0] + deriv_x[:, 1]], 1)
    bending = jnp.stack([deriv_x[:, 3], deriv_y[:, 4], deriv_y[:, 3] + deriv_x[:, 4]], 1)
    transverse = jnp.stack([deriv_x[:, 2] + centre[:, 3], deriv_y[:, 2] + centre[:, 4]], 1)
    heights = jnp.array([-0.5, -0.25, 0.0, 0.25, 0.5], jnp.float32)
    through = jnp.array([1.0, 4.0, 2.0, 4.0, 1.0], jnp.float32) / 12.0
    strains = membrane[:, :, None, :] + heights[None, None, :, None] * bending[:, :, None, :]
    elastic = strains - plastic
    stiffness = modulus / (1.0 - POISSON * POISSON)
    trial_stress = jnp.stack([stiffness * (elastic[:, 0] + POISSON * elastic[:, 1]), stiffness * (POISSON * elastic[:, 0] + elastic[:, 1]), stiffness * 0.5 * (1.0 - POISSON) * elastic[:, 2]], 1)
    equivalent = jnp.sqrt((trial_stress[:, 0] - 0.5 * trial_stress[:, 1]) ** 2 + 0.75 * trial_stress[:, 1] ** 2 + 3.0 * trial_stress[:, 2] ** 2)
    shear_three = 1.5 * modulus / (1.0 + POISSON)
    initial_yield = YIELD + SATURATE * (1.0 - jnp.exp(-RATE * harden))
    step_size = jnp.zeros_like(equivalent)
    for newton_turn in range(NEWTON):
        hardness = harden + step_size
        decay_term = jnp.exp(-RATE * hardness)
        mismatch = equivalent - shear_three * step_size - YIELD - SATURATE * (1.0 - decay_term)
        tangent = shear_three + SATURATE * RATE * decay_term
        active = (newton_turn < costs)[:, None, None]
        step_size = jnp.where(active, step_size + mismatch / tangent, step_size)
    step_size = jnp.where(equivalent > initial_yield, step_size, 0.0)
    shrink = 1.0 - shear_three * step_size / jnp.maximum(equivalent, YIELD)
    stresses = shrink[:, None] * trial_stress
    plastic_new = plastic + (1.0 - shrink)[:, None] * elastic
    harden_new = harden + step_size
    membrane_force = lax.optimization_barrier(jnp.sum(through[None, None, :, None] * stresses, axis=2))
    moments = lax.optimization_barrier(jnp.sum((through * heights)[None, None, :, None] * stresses, axis=2))
    shear_modulus = 5.0 / 6.0 * lax.optimization_barrier(jnp.sum(through[None, :, None] * modulus, axis=1)) / (2.0 * (1.0 + POISSON))
    shear_force = shear_modulus[:, None, :] * transverse
    weight_x = jnp.array([-0.5, 0.5, 0.5, -0.5], jnp.float32)[None, :, None]
    weight_y = jnp.array([-0.5, -0.5, 0.5, 0.5], jnp.float32)[None, :, None]
    force_u = inverse * (weight_x * membrane_force[:, 0:1] + weight_y * membrane_force[:, 2:3])
    force_v = inverse * (weight_y * membrane_force[:, 1:2] + weight_x * membrane_force[:, 2:3])
    force_w = inverse * (weight_x * shear_force[:, 0:1] + weight_y * shear_force[:, 1:2])
    force_a = inverse * (weight_x * moments[:, 0:1] + weight_y * moments[:, 2:3]) + 0.25 * shear_force[:, 0:1]
    force_b = inverse * (weight_y * moments[:, 1:2] + weight_x * moments[:, 2:3]) + 0.25 * shear_force[:, 1:2]
    forces = jnp.stack([force_u, force_v, force_w, force_a, force_b], 1)
    return (forces, plastic_new, harden_new)

def reference(displacement, velocity, nodal_load, nodal_mass, plastic_strain, hardening, ply_modulus, inverse_size, cost_map, migration_plan, block_nodes, corner_slot):
    spans = displacement.shape[0]
    group_nodes = displacement.shape[2]
    blocks = plastic_strain.shape[1]
    points = plastic_strain.shape[3]
    elements = plastic_strain.shape[4]
    window = block_nodes.shape[2]
    extended_nodes = group_nodes + window
    corner_node = jnp.take_along_axis(block_nodes, corner_slot.reshape(spans, blocks, 4 * elements).astype(jnp.int32), axis=2)
    span_index = jnp.arange(spans, dtype=jnp.int32)
    flat_index = (span_index[:, None, None] * extended_nodes + corner_node).reshape(-1).astype(jnp.int32)
    plastic = plastic_strain.reshape(spans * blocks, 3, points, elements)
    harden = hardening.reshape(spans * blocks, points, elements)
    modulus = ply_modulus.reshape(spans * blocks, points, elements)
    inverse = inverse_size.reshape(spans * blocks, elements)
    costs = cost_map.reshape(-1)
    root = (span_index[:, None, None] == 0) & (jnp.arange(group_nodes)[None, None, :] < window)
    disp_now = displacement
    vel_now = velocity
    for time_step in range(STEPS):
        beyond = jnp.concatenate([disp_now[1:, :, :window], jnp.zeros((1, 5, window), jnp.float32)], 0)
        extended = jnp.concatenate([disp_now, beyond], 2)
        table = jnp.transpose(extended, (0, 2, 1)).reshape(spans * extended_nodes, 5)
        corner_disp = table[flat_index].reshape(spans * blocks, 4, elements, 5)
        corner_disp = jnp.transpose(corner_disp, (0, 3, 1, 2))
        forces, plastic, harden = element_update(corner_disp, inverse, modulus, plastic, harden, costs)
        corner_forces = jnp.transpose(forces, (0, 2, 3, 1)).reshape(-1, 5)
        assembled = jax.ops.segment_sum(corner_forces, flat_index, num_segments=spans * extended_nodes)
        assembled = jnp.transpose(assembled.reshape(spans, extended_nodes, 5), (0, 2, 1))
        carried = jnp.concatenate([jnp.zeros((1, 5, window), jnp.float32), assembled[:-1, :, group_nodes:]], 0)
        carried = jnp.pad(carried, ((0, 0), (0, 0), (0, group_nodes - window)))
        internal = assembled[:, :, :group_nodes] + carried
        accel = (nodal_load - internal) / nodal_mass[:, None, :]
        vel_now = jnp.where(root, 0.0, vel_now + STEP_TIME * accel)
        disp_now = disp_now + STEP_TIME * vel_now
    per_device = blocks // N_GRP
    dests = migration_plan[:, :, 0].reshape(spans, N_GRP, per_device)
    earlier = jnp.arange(per_device)[:, None] > jnp.arange(per_device)[None, :]
    same = dests[:, :, :, None] == dests[:, :, None, :]
    rank = lax.optimization_barrier(jnp.sum(same & earlier[None, None], axis=3)).astype(jnp.int32)
    target = (dests * (N_GRP * CAP) + jnp.arange(N_GRP, dtype=jnp.int32)[None, :, None] * CAP + rank).astype(jnp.int32)
    rows = span_index[:, None, None]
    out_plastic = jnp.zeros((spans, N_GRP * N_GRP * CAP, 3, points, elements), jnp.float32)
    out_plastic = out_plastic.at[rows, target].set(plastic.reshape(spans, N_GRP, per_device, 3, points, elements))
    out_harden = jnp.zeros((spans, N_GRP * N_GRP * CAP, points, elements), jnp.float32)
    out_harden = out_harden.at[rows, target].set(harden.reshape(spans, N_GRP, per_device, points, elements))
    return (disp_now, vel_now, out_plastic, out_harden)
```

```python
import jax
import jax.numpy as jnp
from jax import lax
from jax.experimental import pallas as pl
from jax.experimental.pallas import tpu as pltpu
from jax.sharding import PartitionSpec as P

NEWTON = 4
STEPS = 4
POISSON = 0.3
YIELD = 0.1
SATURATE = 0.1
RATE = 20.0
STEP_TIME = 0.25
HEIGHTS = (-0.5, -0.25, 0.0, 0.25, 0.5)
THROUGH = (1.0 / 12, 4.0 / 12, 2.0 / 12, 4.0 / 12, 1.0 / 12)

OWN = 16
LEFT = 12
RIGHT = 9
BLOCKS = LEFT + OWN + RIGHT
ROWS = 40
NROW = 20
NPAD = 24
COMP = 31
PL_ROWS = 472
PR_ROWS = 376
C_H, C_M, C_Z, C_I, C_C = 15, 20, 25, 26, 30
F32 = jnp.float32
BF16 = jnp.bfloat16


def shift(shard, by):
    size = lax.axis_size(("span", "grp"))
    pairs = [(i, i + by) for i in range(size) if 0 <= i + by < size]
    return lax.ppermute(shard, ("span", "grp"), pairs)


def lanes(values, index):
    return jnp.take_along_axis(values, index, axis=1)


def pack_kernel(cost, nodes, slots, pst, hrd, mod, inv, dis, vel, load, mass, to_right, to_left, own):
    first = lax.axis_index("grp") * OWN
    for j in range(OWN):
        own[4, j : j + 1, :] = jnp.full((1, 128), cost[first + j], jnp.int32).astype(F32)
    for o in range(2):
        rows = slice(8 * o, 8 * o + 8)
        low, high = nodes[rows, 0:128], nodes[rows, 128:256]
        base = (first + 8 * o + lax.broadcasted_iota(jnp.int32, (8, 128), 0)) * 64
        for k in range(4):
            slot = slots[rows, k, :]
            lane = slot & 127
            node = jnp.where(slot < 128, lanes(low, lane), lanes(high, lane))
            own[k, rows, :] = (node - base).astype(F32)

    def rows_of(c, at, count):
        if c < 15:
            return pst[c // 5, c % 5, at : at + count, :]
        if c < 20:
            return hrd[c - 15, at : at + count, :]
        if c < 25:
            return mod[c - 20, at : at + count, :]
        if c == 25:
            return inv[at : at + count, :]
        return own[c - 26, at : at + count, :]

    for c in range(COMP):
        to_right[c * LEFT : (c + 1) * LEFT, :] = rows_of(c, OWN - LEFT, LEFT)
        to_left[c * RIGHT : (c + 1) * RIGHT, :] = rows_of(c, 0, RIGHT)
    for i in range(16):
        source = (dis, vel, load)[i // 5] if i < 15 else mass
        values = source[i % 5] if i < 15 else source[...]
        to_right[COMP * LEFT + 6 * i : COMP * LEFT + 6 * i + 6, :] = values[2:8]
        to_left[COMP * RIGHT + 6 * i : COMP * RIGHT + 6 * i + 6, :] = values[0:6]


def element_octet(disp, state, consts, costs, inv):
    half = 0.5 * inv
    dx = [half * (u[1] + u[2] - u[0] - u[3]) for u in disp]
    dy = [half * (u[2] + u[3] - u[0] - u[1]) for u in disp]
    mean_a = 0.25 * (disp[3][0] + disp[3][1] + disp[3][2] + disp[3][3])
    mean_b = 0.25 * (disp[4][0] + disp[4][1] + disp[4][2] + disp[4][3])
    membrane = (dx[0], dy[1], dy[0] + dx[1])
    bending = (dx[3], dy[4], dy[3] + dx[4])
    shear = (dx[2] + mean_a, dy[2] + mean_b)
    active = [costs > float(t) for t in range(NEWTON)]
    new_state = []
    force = [None] * 3
    moment = [None] * 3
    modulus_sum = None
    for p in range(5):
        plastic, harden, modulus = state[p]
        elastic = [membrane[i] + HEIGHTS[p] * bending[i] - plastic[i] for i in range(3)]
        stiff = modulus * (1.0 / (1.0 - POISSON * POISSON))
        t0 = stiff * (elastic[0] + POISSON * elastic[1])
        t1 = stiff * (POISSON * elastic[0] + elastic[1])
        t2 = stiff * (0.5 * (1.0 - POISSON)) * elastic[2]
        s0 = t0 - 0.5 * t1
        q = jnp.sqrt(s0 * s0 + 0.75 * (t1 * t1) + 3.0 * (t2 * t2))
        g3 = modulus * (1.5 / (1.0 + POISSON))
        decay = jnp.exp(-RATE * harden)
        above = q - YIELD - SATURATE * (1.0 - decay)
        plastic_flow = above > 0.0
        step = above / (g3 + SATURATE * RATE * decay)
        for turn in range(1, NEWTON):
            decay = jnp.exp(-RATE * (harden + step))
            miss = q - g3 * step - YIELD - SATURATE * (1.0 - decay)
            step = jnp.where(active[turn], step + miss / (g3 + SATURATE * RATE * decay), step)
        step = jnp.where(plastic_flow, step, 0.0)
        loss = g3 * step / jnp.maximum(q, YIELD)
        keep = 1.0 - loss
        stress = (keep * t0, keep * t1, keep * t2)
        new_state.append(([plastic[i] + loss * elastic[i] for i in range(3)], harden + step))
        for i in range(3):
            part = THROUGH[p] * stress[i]
            force[i] = part if force[i] is None else force[i] + part
            if HEIGHTS[p] != 0.0:
                part = THROUGH[p] * HEIGHTS[p] * stress[i]
                moment[i] = part if moment[i] is None else moment[i] + part
        part = THROUGH[p] * modulus
        modulus_sum = part if modulus_sum is None else modulus_sum + part
    shear_modulus = modulus_sum * (5.0 / 6.0 / (2.0 * (1.0 + POISSON)))
    q0, q1 = shear_modulus * shear[0], shear_modulus * shear[1]
    n = [half * f for f in force]
    m = [half * f for f in moment]
    along_x = (n[0], n[2], half * q0, m[0], m[2])
    along_y = (n[2], n[1], half * q1, m[2], m[1])
    even = (None, None, None, 0.25 * q0, 0.25 * q1)
    return new_state, (along_x, along_y, even)


def step_kernel(
    plan, halo_l, halo_r, own, pst, hrd, mod, inv, dis, vel, load, mass,
    dis_out, vel_out, send,
    st, nd, rm, tab, win, grp, acc, itn,
):
    for c in range(COMP):
        if c < 15:
            mine = pst[c // 5, c % 5]
        elif c < 20:
            mine = hrd[c - 15]
        elif c < 25:
            mine = mod[c - 20]
        elif c == 25:
            mine = inv[...]
        else:
            mine = own[c - 26]
        at = c * ROWS
        st[at : at + LEFT, :] = halo_l[c * LEFT : (c + 1) * LEFT, :]
        st[at + LEFT : at + LEFT + OWN, :] = mine
        st[at + LEFT + OWN : at + BLOCKS, :] = halo_r[c * RIGHT : (c + 1) * RIGHT, :]
        st[at + BLOCKS : at + ROWS, :] = jnp.zeros((ROWS - BLOCKS, 128), F32)
    pinned = (lax.axis_index("span") == 0) & (lax.axis_index("grp") == 0)
    free_rows = jnp.where(
        pinned & (lax.broadcasted_iota(jnp.int32, (8, 128), 0) < 2), 0.0, 1.0
    ).astype(F32)
    for i in range(16):
        left = halo_l[COMP * LEFT + 6 * i : COMP * LEFT + 6 * i + 6, :]
        right = halo_r[COMP * RIGHT + 6 * i : COMP * RIGHT + 6 * i + 6, :]
        if i < 15:
            mine = (dis, vel, load)[i // 5][i % 5]
            if 5 <= i < 10:
                mine = mine * free_rows
            nd[i, 0:6, :] = left
            nd[i, 6:14, :] = mine
            nd[i, 14:20, :] = right
            nd[i, 20:32, :] = jnp.zeros((12, 128), F32)
        else:
            rm[0:6, :] = left
            rm[6:14, :] = mass[...]
            rm[14:20, :] = right
            rm[20:24, :] = jnp.zeros((4, 128), F32)
    weight = rm[...]
    there = weight > 0.0
    weight = jnp.where(there, STEP_TIME / jnp.where(there, weight, 1.0), 0.0)
    rm[...] = weight
    rm[6:14, :] = rm[6:14, :] * free_rows
    grp[...] = jnp.zeros(grp.shape, F32)

    def build(b, _):
        spot = lax.broadcasted_iota(jnp.int32, (256, 128), 0).astype(F32).astype(BF16)
        one, zero = jnp.ones((), BF16), jnp.zeros((), BF16)
        hit = []
        for k in range(4):
            row = st[pl.ds((C_I + k) * ROWS + b, 1), :].astype(BF16)
            hit.append(jnp.where(spot == row, one, zero))
        p, q = hit[1] - hit[3], hit[2] - hit[0]
        tab[b, :, 0:128] = p + q
        tab[b, :, 128:256] = q - p
        tab[b, :, 256:384] = (hit[1] + hit[3]) + (hit[0] + hit[2])
        return 0

    lax.fori_loop(0, ROWS, build, 0)

    lane = lax.broadcasted_iota(jnp.int32, (NPAD, 128), 1)

    def time_step(t, _):
        acc[...] = jnp.zeros(acc.shape, F32)
        for d in range(5):
            here = nd[d, 0:NPAD, :]
            rolled = pltpu.roll(here, 64, 1)
            after = pltpu.roll(nd[d, 1 : NPAD + 1, :], 64, 1)
            win[d, pl.ds(0, NPAD, stride=2), :] = here
            win[d, pl.ds(1, NPAD, stride=2), :] = jnp.where(lane < 64, rolled, after)

        def octet(o, _):
            at = pl.multiple_of(o * 8, 8)

            def comp(c):
                return st[pl.ds(pl.multiple_of(c * ROWS + at, 8), 8), :]

            index = [comp(C_I + k).astype(jnp.int32) for k in range(4)]
            near = [i < 128 for i in index]
            spot = [i & 127 for i in index]
            disp = []
            for d in range(5):
                low = win[d, pl.ds(at, 8), :]
                high = win[d, pl.ds(at + 2, 8), :]
                disp.append([jnp.where(near[k], lanes(low, spot[k]), lanes(high, spot[k])) for k in range(4)])
            state = [([comp(i * 5 + p) for i in range(3)], comp(C_H + p), comp(C_M + p)) for p in range(5)]
            new_state, parts = element_octet(disp, state, None, comp(C_C), comp(C_Z))
            for p in range(5):
                plastic, harden = new_state[p]
                for i in range(3):
                    st[pl.ds(pl.multiple_of((i * 5 + p) * ROWS + at, 8), 8), :] = plastic[i]
                st[pl.ds(pl.multiple_of((C_H + p) * ROWS + at, 8), 8), :] = harden
            for s in range(3):
                for d in range(5):
                    if parts[s][d] is not None:
                        grp[s, pl.ds(d, 8, stride=8), :] = parts[s][d]
            totals = [[None] * 5, [None] * 5]
            for j in range(8):
                values = jnp.concatenate([grp[s, 8 * j : 8 * j + 8, :] for s in range(3)], axis=1)
                high = values.astype(BF16)
                low = (values - high.astype(F32)).astype(BF16)
                both = jnp.concatenate([high, low], axis=0)
                out = lax.dot_general(
                    both, tab[at + j], (((1,), (1,)), ((), ())), preferred_element_type=F32
                )
                out = out[0:8] + out[8:16]
                row = totals[j % 2]
                for h in range(2):
                    piece = out[:, 128 * h : 128 * h + 128]
                    r = j // 2 + h
                    row[r] = piece if row[r] is None else row[r] + piece
            for par in range(2):
                for r in range(5):
                    acc[par, o * 4 + r] = acc[par, o * 4 + r] + totals[par][r]
            return 0

        low_octet = jnp.where(t >= 3, 1, 0)
        high_octet = jnp.where(t >= 2, 4, 5)
        lax.fori_loop(low_octet, high_octet, octet, 0)
        half = lax.broadcasted_iota(jnp.int32, (8, 128), 1) < 64
        before = jnp.zeros((8, 128), F32)
        for r in range(NROW):
            odd = pltpu.roll(acc[1, r], 64, 1)
            itn[pl.ds(r, 8, stride=NPAD), :] = acc[0, r] + jnp.where(half, before, odd)
            before = odd
        weight = rm[...]
        for d in range(5):
            speed = nd[5 + d, 0:NPAD, :] + weight * (nd[10 + d, 0:NPAD, :] - itn[d * NPAD : (d + 1) * NPAD, :])
            nd[5 + d, 0:NPAD, :] = speed
            nd[d, 0:NPAD, :] = nd[d, 0:NPAD, :] + STEP_TIME * speed
        return 0

    itn[...] = jnp.zeros(itn.shape, F32)
    lax.fori_loop(0, STEPS, time_step, 0)
    for d in range(5):
        dis_out[d] = nd[d, 6:14, :]
        vel_out[d] = nd[5 + d, 6:14, :]
    send[...] = jnp.zeros(send.shape, F32)
    first = lax.axis_index("grp") * OWN
    for j in range(OWN):
        send[plan[first + j]] = st[pl.ds(LEFT + j, 20, stride=ROWS), :]


def unpack_kernel(recv, pst, hrd):
    for c in range(20):
        for o in range(4):
            values = recv[8 * o : 8 * o + 8, c, :]
            if c < 15:
                pst[c // 5, c % 5, 8 * o : 8 * o + 8, :] = values
            else:
                hrd[c - 15, 8 * o : 8 * o + 8, :] = values


def vmem(count):
    return [pl.BlockSpec(memory_space=pltpu.VMEM) for _ in range(count)]


def on_device(
    displacement,
    velocity,
    nodal_load,
    nodal_mass,
    plastic_strain,
    hardening,
    ply_modulus,
    inverse_size,
    cost_map,
    migration_plan,
    block_nodes,
    corner_slot,
):
    member = lax.axis_index("grp")
    dis = displacement.reshape(5, 8, 128)
    vel = velocity.reshape(5, 8, 128)
    load = nodal_load.reshape(5, 8, 128)
    mass = nodal_mass.reshape(8, 128)
    pst = jnp.transpose(plastic_strain[0], (1, 2, 0, 3))
    hrd = jnp.transpose(hardening[0], (1, 0, 2))
    mod = jnp.transpose(ply_modulus[0], (1, 0, 2))
    inv = inverse_size[0]
    nodes = lax.dynamic_slice_in_dim(block_nodes[0], member * OWN, OWN, 0)
    slots = lax.dynamic_slice_in_dim(corner_slot[0], member * OWN, OWN, 0)
    smem = pl.BlockSpec(memory_space=pltpu.SMEM)
    to_right, to_left, own = pl.pallas_call(
        pack_kernel,
        out_shape=(
            jax.ShapeDtypeStruct((PL_ROWS, 128), F32),
            jax.ShapeDtypeStruct((PR_ROWS, 128), F32),
            jax.ShapeDtypeStruct((5, OWN, 128), F32),
        ),
        in_specs=[smem] + vmem(10),
        out_specs=tuple(vmem(3)),
        name="pack",
    )(cost_map[0], nodes, slots, pst, hrd, mod, inv, dis, vel, load, mass)
    halo_l = shift(to_right, 1)
    halo_r = shift(to_left, -1)
    dis_out, vel_out, send = pl.pallas_call(
        step_kernel,
        out_shape=(
            jax.ShapeDtypeStruct((5, 8, 128), F32),
            jax.ShapeDtypeStruct((5, 8, 128), F32),
            jax.ShapeDtypeStruct((32, 20, 128), F32),
        ),
        in_specs=[smem] + vmem(11),
        out_specs=tuple(vmem(3)),
        scratch_shapes=[
            pltpu.VMEM((COMP * ROWS, 128), F32),
            pltpu.VMEM((15, 32, 128), F32),
            pltpu.VMEM((NPAD, 128), F32),
            pltpu.VMEM((ROWS, 256, 384), BF16),
            pltpu.VMEM((5, 56, 128), F32),
            pltpu.VMEM((3, 64, 128), F32),
            pltpu.VMEM((2, NPAD, 8, 128), F32),
            pltpu.VMEM((8 * NPAD, 128), F32),
        ],
        compiler_params=pltpu.CompilerParams(vmem_limit_bytes=40 << 20),
        name="steps",
    )(migration_plan[0, :, 0], halo_l, halo_r, own, pst, hrd, mod, inv, dis, vel, load, mass)
    recv = lax.all_to_all(send, "grp", split_axis=0, concat_axis=0, tiled=True)
    res_p, res_h = pl.pallas_call(
        unpack_kernel,
        out_shape=(
            jax.ShapeDtypeStruct((3, 5, 32, 128), F32),
            jax.ShapeDtypeStruct((5, 32, 128), F32),
        ),
        in_specs=vmem(1),
        out_specs=tuple(vmem(2)),
        name="unpack",
    )(recv)
    return (
        dis_out.reshape(1, 5, 1024),
        vel_out.reshape(1, 5, 1024),
        jnp.transpose(res_p, (2, 0, 1, 3))[None],
        jnp.transpose(res_h, (1, 0, 2))[None],
    )


def solution(mesh):
    return jax.shard_map(
        on_device,
        mesh=mesh,
        in_specs=(
            P("span", None, "grp"),
            P("span", None, "grp"),
            P("span", None, "grp"),
            P("span", "grp"),
            P("span", "grp", None, None, None),
            P("span", "grp", None, None),
            P("span", "grp", None, None),
            P("span", "grp", None),
            P("span", None),
            P("span", None, None),
            P("span", None, None),
            P("span", None, None, None),
        ),
        out_specs=(
            P("span", None, "grp"),
            P("span", None, "grp"),
            P("span", "grp", None, None, None),
            P("span", "grp", None, None),
        ),
        check_vma=False,
    )
```

```python
import math

import jax
import jax.numpy as jnp
from jax import lax
from jax.experimental import pallas as pl
from jax.experimental.pallas import tpu as pltpu
from jax.sharding import PartitionSpec as P

NEWTON = 4
STEPS = 4
POISSON = 0.3
YIELD = 0.1
SATURATE = 0.1
RATE = 20.0
STEP_TIME = 0.25
THROUGH = (1.0 / 12, 4.0 / 12, 2.0 / 12, 4.0 / 12, 1.0 / 12)

OWN = 16
LEFT = 12
RIGHT = 9
BLOCKS = LEFT + OWN + RIGHT
ROWS = 40
NROW = 20
NPAD = 24
COMP = 31
PL_ROWS = 472
PR_ROWS = 376
C_H, C_M, C_Z, C_I, C_C = 15, 20, 25, 26, 30
F32 = jnp.float32
BF16 = jnp.bfloat16


def shift(shard, by):
    size = lax.axis_size(("span", "grp"))
    pairs = [(i, i + by) for i in range(size) if 0 <= i + by < size]
    return lax.ppermute(shard, ("span", "grp"), pairs)


def lanes(values, index):
    return jnp.take_along_axis(values, index, axis=1)


def pack_kernel(
    cost, nodes_all, slots_all, pst, hrd, mod, inv, dis, vel, load, mass,
    to_right, to_left, own,
    nodes, slots, sems,
):
    first = pl.multiple_of(lax.axis_index("grp") * OWN, OWN)
    fetch_nodes = pltpu.make_async_copy(nodes_all.at[pl.ds(first, OWN)], nodes, sems.at[0])
    fetch_slots = pltpu.make_async_copy(slots_all.at[pl.ds(first, OWN)], slots, sems.at[1])
    fetch_nodes.start()
    fetch_slots.start()
    for j in range(OWN):
        own[4, j : j + 1, :] = jnp.full((1, 128), cost[first + j], jnp.int32).astype(F32)
    def rows_of(c, at, count):
        if c < 15:
            return pst[c // 5, c % 5, at : at + count, :]
        if c < 20:
            return hrd[c - 15, at : at + count, :]
        if c < 25:
            return mod[c - 20, at : at + count, :]
        if c == 25:
            return inv[at : at + count, :]
        return own[c - 26, at : at + count, :]

    for c in range(C_I):
        to_right[c * LEFT : (c + 1) * LEFT, :] = rows_of(c, OWN - LEFT, LEFT)
        to_left[c * RIGHT : (c + 1) * RIGHT, :] = rows_of(c, 0, RIGHT)
    for i in range(16):
        source = (dis, vel, load)[i // 5] if i < 15 else mass
        values = source[i % 5] if i < 15 else source[...]
        to_right[COMP * LEFT + 6 * i : COMP * LEFT + 6 * i + 6, :] = values[2:8]
        to_left[COMP * RIGHT + 6 * i : COMP * RIGHT + 6 * i + 6, :] = values[0:6]
    fetch_nodes.wait()
    fetch_slots.wait()
    for o in range(2):
        rows = slice(8 * o, 8 * o + 8)
        low, high = nodes[rows, 0:128], nodes[rows, 128:256]
        base = (first + 8 * o + lax.broadcasted_iota(jnp.int32, (8, 128), 0)) * 64
        for k in range(4):
            slot = slots[rows, k, :]
            lane = slot & 127
            node = jnp.where(slot < 128, lanes(low, lane), lanes(high, lane))
            own[k, rows, :] = (node - base).astype(F32)

    for c in range(C_I, COMP):
        to_right[c * LEFT : (c + 1) * LEFT, :] = rows_of(c, OWN - LEFT, LEFT)
        to_left[c * RIGHT : (c + 1) * RIGHT, :] = rows_of(c, 0, RIGHT)


SLOPE = -RATE * math.log2(math.e)
DIAG = 1.0 - POISSON + POISSON * POISSON
CROSS = (4.0 * POISSON - 1.0 - POISSON * POISSON) / DIAG
SHEAR = 3.0 * (0.5 * (1.0 - POISSON)) ** 2 / DIAG
ELASTIC = 1.0 / (1.0 - POISSON * POISSON)
TRIPLE = 1.5 / (1.0 + POISSON)


def element_octet(disp, state, costs, inv):
    half = 0.5 * inv
    lean = [u[1] - u[3] for u in disp]
    rise = [u[2] - u[0] for u in disp]
    dx = [half * (s + t) for s, t in zip(lean, rise)]
    dy = [half * (t - s) for s, t in zip(lean, rise)]
    mean_a = 0.25 * ((disp[3][0] + disp[3][1]) + (disp[3][2] + disp[3][3]))
    mean_b = 0.25 * ((disp[4][0] + disp[4][1]) + (disp[4][2] + disp[4][3]))
    membrane = (dx[0], dy[1], dy[0] + dx[1])
    bending = (dx[3], dy[4], dy[3] + dx[4])
    shear = (dx[2] + mean_a, dy[2] + mean_b)
    far = [0.5 * b for b in bending]
    near = [0.25 * b for b in bending]
    fibre = (
        [m - b for m, b in zip(membrane, far)],
        [m - b for m, b in zip(membrane, near)],
        membrane,
        [m + b for m, b in zip(membrane, near)],
        [m + b for m, b in zip(membrane, far)],
    )
    active = [costs > float(t) for t in range(NEWTON)]
    offset = 0.5 * SATURATE * SLOPE
    new_state = []
    load = []
    g3_sum = None
    for p in range(5):
        plastic, level, g3 = state[p]
        e0, e1, e2 = [fibre[p][i] - plastic[i] for i in range(3)]
        square = e1 * (e1 + CROSS * e0) + e0 * e0 + SHEAR * (e2 * e2)
        norm = square * lax.rsqrt(jnp.maximum(square, 1e-37))
        q = (g3 * norm) * (SLOPE * ELASTIC / TRIPLE * math.sqrt(DIAG))
        base = q - SLOPE * (YIELD + SATURATE)
        decay = jnp.exp2(level)
        top = base + offset * decay
        flows = top < 0.0
        step = top / (g3 + decay)
        for turn in range(1, NEWTON):
            decay = jnp.exp2(level + step)
            moved = (base + decay * (step + offset)) / (g3 + decay)
            step = jnp.where(active[turn], moved, step)
        step = jnp.where(flows, step, 0.0)
        loss = (g3 * step) / jnp.minimum(q, SLOPE * YIELD)
        new_state.append(([plastic[0] + loss * e0, plastic[1] + loss * e1, plastic[2] + loss * e2], level + step))
        scale = (g3 * (THROUGH[p] * ELASTIC / TRIPLE)) * (1.0 - loss)
        load.append([scale * e0, scale * e1, scale * e2])
        part = THROUGH[p] * g3
        g3_sum = part if g3_sum is None else g3_sum + part
    force = [((load[0][i] + load[4][i]) + (load[1][i] + load[3][i])) + load[2][i] for i in range(3)]
    moment = [0.5 * (load[4][i] - load[0][i]) + 0.25 * (load[3][i] - load[1][i]) for i in range(3)]

    def resultant(s):
        a, b, c = half * s[0], half * s[1], half * s[2]
        return a + POISSON * b, POISSON * a + b, (0.5 * (1.0 - POISSON)) * c

    shear_modulus = g3_sum * (5.0 / 6.0 / (2.0 * (1.0 + POISSON)) / TRIPLE)
    q0, q1 = shear_modulus * shear[0], shear_modulus * shear[1]
    n0, n1, n2 = resultant(force)
    m0, m1, m2 = resultant(moment)
    k0, k1 = half * q0, half * q1
    lean_part = (n0 - n2, n2 - n1, k0 - k1, m0 - m2, m2 - m1)
    rise_part = (n0 + n2, n2 + n1, k0 + k1, m0 + m2, m2 + m1)
    even = (None, None, None, 0.25 * q0, 0.25 * q1)
    return new_state, (lean_part, rise_part, even)


def build_tables(corner_row, count, tab, spot, off):
    spot[...] = lax.broadcasted_iota(jnp.int32, (256, 256), 0).astype(F32).astype(BF16)

    def spread(b, _):
        for k, place in ((1, 0), (2, 1), (3, 2), (0, 3)):
            row = jnp.broadcast_to(corner_row(k, b), (8, 128))
            off[b, :, 128 * place : 128 * place + 128] = row.astype(BF16)
        return 0

    lax.fori_loop(0, count, spread, 0, unroll=min(4, count) if count % 4 == 0 else 3)

    def build(b, _):
        one, zero = jnp.ones((8, 256), BF16), jnp.zeros((8, 256), BF16)
        first, second = off[b, :, 0:256], off[b, :, 256:512]
        for r in range(32):
            rows = slice(8 * r, 8 * r + 8)
            here = spot[rows, :]
            hit = jnp.where(here == first, one, zero)
            miss = jnp.where(here == second, one, zero)
            tab[b, rows, 0:256] = hit - miss
            both = hit + miss
            tab[b, rows, 256:384] = both[:, 0:128] + both[:, 128:256]
        return 0

    lax.fori_loop(0, count, build, 0)


def table_kernel(own, tab, spot, off):
    build_tables(lambda k, b: own[k, pl.ds(b, 1), :], OWN, tab, spot, off)


def step_kernel(
    plan, halo_l, halo_r, own, tab_own, pst, hrd, mod, inv, dis, vel, load, mass,
    dis_out, vel_out, send,
    st, nd, rm, tab, win, grp, itn, spot, off,
):
    for c in range(COMP):
        if c < 15:
            mine = pst[c // 5, c % 5]
        elif c < 20:
            mine = hrd[c - 15]
        elif c < 25:
            mine = mod[c - 20]
        elif c == 25:
            mine = inv[...]
        else:
            mine = own[c - 26]
        at = c * ROWS
        scale, bias = 1.0, 0.0
        if C_H <= c < C_M:
            scale, bias = SLOPE, 1.0
        elif C_M <= c < C_Z:
            scale = TRIPLE
        st[at : at + LEFT, :] = halo_l[c * LEFT : (c + 1) * LEFT, :] * scale + bias
        st[at + LEFT : at + LEFT + OWN, :] = mine * scale + bias
        st[at + LEFT + OWN : at + BLOCKS, :] = halo_r[c * RIGHT : (c + 1) * RIGHT, :] * scale + bias
        st[at + BLOCKS : at + ROWS, :] = jnp.zeros((ROWS - BLOCKS, 128), F32)
    pinned = (lax.axis_index("span") == 0) & (lax.axis_index("grp") == 0)
    free_rows = jnp.where(
        pinned & (lax.broadcasted_iota(jnp.int32, (8, 128), 0) < 2), 0.0, 1.0
    ).astype(F32)
    for i in range(16):
        left = halo_l[COMP * LEFT + 6 * i : COMP * LEFT + 6 * i + 6, :]
        right = halo_r[COMP * RIGHT + 6 * i : COMP * RIGHT + 6 * i + 6, :]
        if i < 15:
            mine = (dis, vel, load)[i // 5][i % 5]
            if 5 <= i < 10:
                mine = mine * free_rows
            nd[i, 0:6, :] = left
            nd[i, 6:14, :] = mine
            nd[i, 14:20, :] = right
            nd[i, 20:32, :] = jnp.zeros((12, 128), F32)
        else:
            rm[0:6, :] = left
            rm[6:14, :] = mass[...]
            rm[14:20, :] = right
            rm[20:24, :] = jnp.zeros((4, 128), F32)
    weight = rm[...]
    there = weight > 0.0
    weight = jnp.where(there, STEP_TIME / jnp.where(there, weight, 1.0), 0.0)
    rm[...] = weight
    rm[6:14, :] = rm[6:14, :] * free_rows
    grp[...] = jnp.zeros(grp.shape, F32)

    def halo_row(k, b):
        return st[pl.ds((C_I + k) * ROWS + jnp.where(b < LEFT, b, b + OWN), 1), :]

    build_tables(halo_row, LEFT + RIGHT, tab, spot, off)

    def table(b):
        if b < LEFT:
            return tab[b]
        return tab_own[b - LEFT] if b < LEFT + OWN else tab[b - OWN]

    lane = lax.broadcasted_iota(jnp.int32, (NPAD, 128), 1)

    half_lane = lax.broadcasted_iota(jnp.int32, (8, 128), 1) < 64

    def comp(c, o):
        return st[c * ROWS + 8 * o : c * ROWS + 8 * o + 8, :]

    def update(o):
        at = 8 * o
        index = [comp(C_I + k, o).astype(jnp.int32) for k in range(4)]
        near = [i < 128 for i in index]
        place = [i & 127 for i in index]
        disp = []
        for d in range(5):
            low = win[d, at : at + 8, :]
            high = win[d, at + 2 : at + 10, :]
            disp.append([jnp.where(near[k], lanes(low, place[k]), lanes(high, place[k])) for k in range(4)])
        state = [([comp(i * 5 + p, o) for i in range(3)], comp(C_H + p, o), comp(C_M + p, o)) for p in range(5)]
        new_state, parts = element_octet(disp, state, comp(C_C, o), comp(C_Z, o))
        for p in range(5):
            plastic, level = new_state[p]
            for i in range(3):
                st[(i * 5 + p) * ROWS + at : (i * 5 + p) * ROWS + at + 8, :] = plastic[i]
            st[(C_H + p) * ROWS + at : (C_H + p) * ROWS + at + 8, :] = level
        for s in range(3):
            for d in range(5):
                if parts[s][d] is not None:
                    grp[o, s, pl.ds(d, 8, stride=8), :] = parts[s][d]

    def assemble(o, totals, first, last):
        for j in range(8):
            b = 8 * o + j
            if not first <= b < last:
                continue
            values = jnp.concatenate([grp[o, s, 8 * j : 8 * j + 8, :] for s in range(3)], axis=1)
            high = values.astype(BF16)
            low = (values - high.astype(F32)).astype(BF16)
            both = jnp.concatenate([high, low], axis=0)
            out = lax.dot_general(both, table(b), (((1,), (1,)), ((), ())), preferred_element_type=F32)
            out = out[0:8] + out[8:16]
            for h in range(2):
                piece = out[:, 128 * h : 128 * h + 128]
                place = (j % 2, b // 2 + h)
                totals[place] = piece if place not in totals else totals[place] + piece

    itn[...] = jnp.zeros(itn.shape, F32)
    for t in range(STEPS):
        reach_l, reach_r = 3 * (STEPS - t), 3 * (STEPS - t - 1)
        first, last = LEFT - reach_l, LEFT + OWN + reach_r
        for d in range(5):
            here = nd[d, 0:NPAD, :]
            rolled = pltpu.roll(here, 64, 1)
            after = pltpu.roll(nd[d, 1 : NPAD + 1, :], 64, 1)
            win[d, pl.ds(0, NPAD, stride=2), :] = here
            win[d, pl.ds(1, NPAD, stride=2), :] = jnp.where(lane < 64, rolled, after)
        totals = {}
        for o in range(first // 8, (last + 7) // 8):
            update(o)
            assemble(o, totals, first, last)
        zero = jnp.zeros((8, 128), F32)
        before = zero
        for r in range(NROW):
            odd = pltpu.roll(totals[1, r], 64, 1) if (1, r) in totals else zero
            itn[pl.ds(r, 8, stride=NPAD), :] = totals.get((0, r), zero) + jnp.where(half_lane, before, odd)
            before = odd
        weight = rm[...]
        for d in range(5):
            speed = nd[5 + d, 0:NPAD, :] + weight * (nd[10 + d, 0:NPAD, :] - itn[d * NPAD : (d + 1) * NPAD, :])
            nd[5 + d, 0:NPAD, :] = speed
            nd[d, 0:NPAD, :] = nd[d, 0:NPAD, :] + STEP_TIME * speed

    for d in range(5):
        dis_out[d] = nd[d, 6:14, :]
        vel_out[d] = nd[5 + d, 6:14, :]
    send[...] = jnp.zeros(send.shape, F32)
    for p in range(5):
        rows = slice((C_H + p) * ROWS + LEFT, (C_H + p) * ROWS + LEFT + OWN)
        st[rows, :] = (st[rows, :] - 1.0) * (1.0 / SLOPE)
    first = lax.axis_index("grp") * OWN
    for j in range(OWN):
        for q in range(5):
            send[plan[first + j], q] = st[pl.ds(4 * q * ROWS + LEFT + j, 4, stride=ROWS), :]


def unpack_kernel(recv, pst, hrd):
    for g in range(32):
        for q in range(5):
            values = recv[g, q]
            if q < 3:
                pst[pl.ds(128 * q + g, 4, stride=32), :] = values
            elif q == 3:
                pst[pl.ds(384 + g, 3, stride=32), :] = values[0:3]
                hrd[pl.ds(g, 1), :] = values[3:4]
            else:
                hrd[pl.ds(32 + g, 4, stride=32), :] = values


def vmem(count):
    return [pl.BlockSpec(memory_space=pltpu.VMEM) for _ in range(count)]


def on_device(
    displacement,
    velocity,
    nodal_load,
    nodal_mass,
    plastic_strain,
    hardening,
    ply_modulus,
    inverse_size,
    cost_map,
    migration_plan,
    block_nodes,
    corner_slot,
):
    dis = displacement.reshape(5, 8, 128)
    vel = velocity.reshape(5, 8, 128)
    load = nodal_load.reshape(5, 8, 128)
    mass = nodal_mass.reshape(8, 128)
    pst = jnp.transpose(plastic_strain[0], (1, 2, 0, 3))
    hrd = jnp.transpose(hardening[0], (1, 0, 2))
    mod = jnp.transpose(ply_modulus[0], (1, 0, 2))
    inv = inverse_size[0]
    smem = pl.BlockSpec(memory_space=pltpu.SMEM)
    hbm = pl.BlockSpec(memory_space=pltpu.HBM)
    to_right, to_left, own = pl.pallas_call(
        pack_kernel,
        out_shape=(
            jax.ShapeDtypeStruct((PL_ROWS, 128), F32),
            jax.ShapeDtypeStruct((PR_ROWS, 128), F32),
            jax.ShapeDtypeStruct((5, OWN, 128), F32),
        ),
        in_specs=[smem, hbm, hbm] + vmem(8),
        out_specs=tuple(vmem(3)),
        scratch_shapes=[
            pltpu.VMEM((OWN, 256), jnp.int32),
            pltpu.VMEM((OWN, 4, 128), jnp.int32),
            pltpu.SemaphoreType.DMA((2,)),
        ],
        compiler_params=pltpu.CompilerParams(vmem_limit_bytes=60 * 1024 * 1024),
        name="pack",
    )(cost_map[0], block_nodes[0], corner_slot[0], pst, hrd, mod, inv, dis, vel, load, mass)
    tab_own = pl.pallas_call(
        table_kernel,
        out_shape=jax.ShapeDtypeStruct((OWN, 256, 384), BF16),
        in_specs=vmem(1),
        out_specs=vmem(1)[0],
        scratch_shapes=[pltpu.VMEM((256, 256), BF16), pltpu.VMEM((OWN, 8, 512), BF16)],
        compiler_params=pltpu.CompilerParams(vmem_limit_bytes=8 << 20),
        cost_estimate=pl.CostEstimate(flops=20_000_000, bytes_accessed=6_000_000, transcendentals=0),
        name="tables",
    )(own)
    halo_l = shift(to_right, 1)
    halo_r = shift(to_left, -1)
    dis_out, vel_out, send = pl.pallas_call(
        step_kernel,
        out_shape=(
            jax.ShapeDtypeStruct((5, 8, 128), F32),
            jax.ShapeDtypeStruct((5, 8, 128), F32),
            jax.ShapeDtypeStruct((32, 5, 4, 128), F32),
        ),
        in_specs=[smem] + vmem(12),
        out_specs=tuple(vmem(3)),
        scratch_shapes=[
            pltpu.VMEM((COMP * ROWS, 128), F32),
            pltpu.VMEM((15, 32, 128), F32),
            pltpu.VMEM((NPAD, 128), F32),
            pltpu.VMEM((LEFT + RIGHT, 256, 384), BF16),
            pltpu.VMEM((5, 56, 128), F32),
            pltpu.VMEM((ROWS // 8, 3, 64, 128), F32),
            pltpu.VMEM((8 * NPAD, 128), F32),
            pltpu.VMEM((256, 256), BF16),
            pltpu.VMEM((LEFT + RIGHT, 8, 512), BF16),
        ],
        compiler_params=pltpu.CompilerParams(vmem_limit_bytes=24 << 20),
        name="steps",
    )(migration_plan[0, :, 0], halo_l, halo_r, own, tab_own, pst, hrd, mod, inv, dis, vel, load, mass)
    recv = lax.all_to_all(send, "grp", split_axis=0, concat_axis=0, tiled=True)
    res_p, res_h = pl.pallas_call(
        unpack_kernel,
        out_shape=(
            jax.ShapeDtypeStruct((480, 128), F32),
            jax.ShapeDtypeStruct((160, 128), F32),
        ),
        in_specs=vmem(1),
        out_specs=tuple(vmem(2)),
        compiler_params=pltpu.CompilerParams(vmem_limit_bytes=4 << 20),
        name="unpack",
    )(recv)
    return (
        dis_out.reshape(1, 5, 1024),
        vel_out.reshape(1, 5, 1024),
        jnp.transpose(res_p.reshape(3, 5, 32, 128), (2, 0, 1, 3))[None],
        jnp.transpose(res_h.reshape(5, 32, 128), (1, 0, 2))[None],
    )


def solution(mesh):
    return jax.shard_map(
        on_device,
        mesh=mesh,
        in_specs=(
            P("span", None, "grp"),
            P("span", None, "grp"),
            P("span", None, "grp"),
            P("span", "grp"),
            P("span", "grp", None, None, None),
            P("span", "grp", None, None),
            P("span", "grp", None, None),
            P("span", "grp", None),
            P("span", None),
            P("span", None, None),
            P("span", None, None),
            P("span", None, None, None),
        ),
        out_specs=(
            P("span", None, "grp"),
            P("span", None, "grp"),
            P("span", "grp", None, None, None),
            P("span", "grp", None, None),
        ),
        check_vma=False,
    )
```

```python
import math

import jax
import jax.numpy as jnp
from jax import lax
from jax.experimental import pallas as pl
from jax.experimental.pallas import tpu as pltpu
from jax.sharding import PartitionSpec as P

NEWTON = 4
STEPS = 4
POISSON = 0.3
YIELD = 0.1
SATURATE = 0.1
RATE = 20.0
STEP_TIME = 0.25
THROUGH = (1.0 / 12, 4.0 / 12, 2.0 / 12, 4.0 / 12, 1.0 / 12)

OWN = 16
LEFT = 12
RIGHT = 9
BLOCKS = LEFT + OWN + RIGHT
ROWS = 40
NROW = 20
NPAD = 24
COMP = 31
PL_ROWS = 472
PR_ROWS = 376
C_H, C_M, C_Z, C_I, C_C = 15, 20, 25, 26, 30
F32 = jnp.float32
BF16 = jnp.bfloat16


def shift(shard, by):
    size = lax.axis_size(("span", "grp"))
    pairs = [(i, i + by) for i in range(size) if 0 <= i + by < size]
    return lax.ppermute(shard, ("span", "grp"), pairs)


def lanes(values, index):
    return jnp.take_along_axis(values, index, axis=1)


def corner_spots(nodes, slots, base, put):
    for o in range(2):
        rows = slice(8 * o, 8 * o + 8)
        low, high = nodes[rows, 0:128], nodes[rows, 128:256]
        start = (base + 8 * o + lax.broadcasted_iota(jnp.int32, (8, 128), 0)) * 64
        for k in range(4):
            slot = slots[rows, k, :]
            lane = slot & 127
            node = jnp.where(slot < 128, lanes(low, lane), lanes(high, lane))
            put(k, o, (node - start).astype(F32))


def pack_kernel(
    cost_all, nodes_all, slots_all, pst_all, hrd_all, mod_all, inv_all, dis_all, vel_all, load_all, mass_all,
    to_right, to_left, own,
    nodes, slots, pst, hrd, mod, inv, dis, vel, load, mass, cost, sems,
):
    first = pl.multiple_of(lax.axis_index("grp") * OWN, OWN)
    total = nodes_all.shape[0]
    starts = (first, jnp.maximum(first - OWN, 0), jnp.minimum(first + OWN, total - OWN))
    lists = []
    for i, start in enumerate(starts):
        rows = pl.ds(pl.multiple_of(start, OWN), OWN)
        lists.append(pltpu.make_async_copy(nodes_all.at[rows], nodes.at[i], sems.at[8 + 2 * i]))
        lists.append(pltpu.make_async_copy(slots_all.at[rows], slots.at[i], sems.at[9 + 2 * i]))
    pairs = (
        (pst_all, pst), (hrd_all, hrd), (mod_all, mod), (inv_all, inv),
        (dis_all, dis), (vel_all, vel), (load_all, load), (mass_all, mass),
    )
    others = [pltpu.make_async_copy(source, target, sems.at[i]) for i, (source, target) in enumerate(pairs)]
    fetch_cost = pltpu.make_async_copy(cost_all, cost, sems.at[14])
    for copy in lists + others + [fetch_cost]:
        copy.start()
    for copy in lists:
        copy.wait()

    def put_own(k, o, values):
        own[k, LEFT + 8 * o : LEFT + 8 * o + 8, :] = values

    def put_left(k, o, values):
        if o == 0:
            own[k, 0:4, :] = values[4:8]
        else:
            own[k, 4:12, :] = values

    def put_right(k, o, values):
        if o == 0:
            own[k, LEFT + OWN : LEFT + OWN + 8, :] = values
        else:
            own[k, LEFT + OWN + 8 : BLOCKS, :] = values[0:1]

    corner_spots(nodes.at[0], slots.at[0], first, put_own)
    corner_spots(nodes.at[1], slots.at[1], first - OWN, put_left)
    corner_spots(nodes.at[2], slots.at[2], first + OWN, put_right)
    for k in range(4):
        own[k, BLOCKS:ROWS, :] = jnp.zeros((ROWS - BLOCKS, 128), F32)
    fetch_cost.wait()
    for j in range(OWN):
        own[4, LEFT + j : LEFT + j + 1, :] = jnp.full((1, 128), cost[first + j], jnp.int32).astype(F32)
    for copy in others:
        copy.wait()

    def rows_of(c, at, count):
        if c < 15:
            return pst[c // 5, c % 5, at : at + count, :]
        if c < 20:
            return hrd[c - 15, at : at + count, :]
        if c < 25:
            return mod[c - 20, at : at + count, :]
        if c == 25:
            return inv[at : at + count, :]
        return own[c - 26, LEFT + at : LEFT + at + count, :]

    for c in range(COMP):
        to_right[c * LEFT : (c + 1) * LEFT, :] = rows_of(c, OWN - LEFT, LEFT)
        to_left[c * RIGHT : (c + 1) * RIGHT, :] = rows_of(c, 0, RIGHT)
    for i in range(16):
        source = (dis, vel, load)[i // 5] if i < 15 else mass
        values = source[i % 5] if i < 15 else source[...]
        to_right[COMP * LEFT + 6 * i : COMP * LEFT + 6 * i + 6, :] = values[2:8]
        to_left[COMP * RIGHT + 6 * i : COMP * RIGHT + 6 * i + 6, :] = values[0:6]


SLOPE = -RATE * math.log2(math.e)
DIAG = 1.0 - POISSON + POISSON * POISSON
CROSS = (4.0 * POISSON - 1.0 - POISSON * POISSON) / DIAG
SHEAR = 3.0 * (0.5 * (1.0 - POISSON)) ** 2 / DIAG
ELASTIC = 1.0 / (1.0 - POISSON * POISSON)
TRIPLE = 1.5 / (1.0 + POISSON)


def element_octet(disp, state, costs, inv):
    half = 0.5 * inv
    lean = [u[1] - u[3] for u in disp]
    rise = [u[2] - u[0] for u in disp]
    dx = [half * (s + t) for s, t in zip(lean, rise)]
    dy = [half * (t - s) for s, t in zip(lean, rise)]
    mean_a = 0.25 * ((disp[3][0] + disp[3][1]) + (disp[3][2] + disp[3][3]))
    mean_b = 0.25 * ((disp[4][0] + disp[4][1]) + (disp[4][2] + disp[4][3]))
    membrane = (dx[0], dy[1], dy[0] + dx[1])
    bending = (dx[3], dy[4], dy[3] + dx[4])
    shear = (dx[2] + mean_a, dy[2] + mean_b)
    far = [0.5 * b for b in bending]
    near = [0.25 * b for b in bending]
    fibre = (
        [m - b for m, b in zip(membrane, far)],
        [m - b for m, b in zip(membrane, near)],
        membrane,
        [m + b for m, b in zip(membrane, near)],
        [m + b for m, b in zip(membrane, far)],
    )
    active = [costs > float(t) for t in range(NEWTON)]
    offset = 0.5 * SATURATE * SLOPE
    new_state = []
    load = []
    g3_sum = None
    for p in range(5):
        plastic, level, g3 = state[p]
        e0, e1, e2 = [fibre[p][i] - plastic[i] for i in range(3)]
        square = e1 * (e1 + CROSS * e0) + e0 * e0 + SHEAR * (e2 * e2)
        norm = square * lax.rsqrt(jnp.maximum(square, 1e-37))
        q = (g3 * norm) * (SLOPE * ELASTIC / TRIPLE * math.sqrt(DIAG))
        base = q - SLOPE * (YIELD + SATURATE)
        decay = jnp.exp2(level)
        top = base + offset * decay
        flows = top < 0.0
        step = top / (g3 + decay)
        for turn in range(1, NEWTON):
            decay = jnp.exp2(level + step)
            moved = (base + decay * (step + offset)) / (g3 + decay)
            step = jnp.where(active[turn], moved, step)
        step = jnp.where(flows, step, 0.0)
        loss = (g3 * step) / jnp.minimum(q, SLOPE * YIELD)
        new_state.append(([plastic[0] + loss * e0, plastic[1] + loss * e1, plastic[2] + loss * e2], level + step))
        scale = (g3 * (THROUGH[p] * ELASTIC / TRIPLE)) * (1.0 - loss)
        load.append([scale * e0, scale * e1, scale * e2])
        part = THROUGH[p] * g3
        g3_sum = part if g3_sum is None else g3_sum + part
    force = [((load[0][i] + load[4][i]) + (load[1][i] + load[3][i])) + load[2][i] for i in range(3)]
    moment = [0.5 * (load[4][i] - load[0][i]) + 0.25 * (load[3][i] - load[1][i]) for i in range(3)]

    def resultant(s):
        a, b, c = half * s[0], half * s[1], half * s[2]
        return a + POISSON * b, POISSON * a + b, (0.5 * (1.0 - POISSON)) * c

    shear_modulus = g3_sum * (5.0 / 6.0 / (2.0 * (1.0 + POISSON)) / TRIPLE)
    q0, q1 = shear_modulus * shear[0], shear_modulus * shear[1]
    n0, n1, n2 = resultant(force)
    m0, m1, m2 = resultant(moment)
    k0, k1 = half * q0, half * q1
    lean_part = (n0 - n2, n2 - n1, k0 - k1, m0 - m2, m2 - m1)
    rise_part = (n0 + n2, n2 + n1, k0 + k1, m0 + m2, m2 + m1)
    even = (None, None, None, 0.25 * q0, 0.25 * q1)
    return new_state, (lean_part, rise_part, even)


def table_octet(rows, turned, put, count=8):
    turned[...] = jnp.transpose(jnp.concatenate(rows + [jnp.zeros((96, 128), F32)], axis=0))
    one, zero = jnp.ones((), BF16), jnp.zeros((), BF16)
    near = lax.broadcasted_iota(jnp.int32, (128, 128), 1).astype(F32)
    spots = (near.astype(BF16), (near + 128.0).astype(BF16))
    for j in range(count):
        column = [
            jnp.broadcast_to(turned[:, 8 * k + j : 8 * k + j + 1], (128, 128)).astype(BF16) for k in range(4)
        ]
        for half in range(2):
            hit = [jnp.where(c == spots[half], one, zero) for c in column]
            side = slice(128 * half, 128 * half + 128)
            put(j, 0, side, hit[1] - hit[3])
            put(j, 128, side, hit[2] - hit[0])
            put(j, 256, side, (hit[1] + hit[3]) + (hit[0] + hit[2]))


def table_kernel(spots, tab, turned):
    def octet(o, _):
        at = pl.multiple_of(o * 8, 8)

        def put(j, row, side, values):
            tab[at + j, row : row + 128, side] = values

        table_octet([spots[k, pl.ds(at, 8), :] for k in range(4)], turned, put)
        return 0

    lax.fori_loop(0, BLOCKS // 8, octet, 0)
    rest = BLOCKS // 8 * 8

    def put_rest(j, row, side, values):
        tab[rest + j, row : row + 128, side] = values

    table_octet([spots[k, rest : rest + 8, :] for k in range(4)], turned, put_rest, BLOCKS - rest)


def step_kernel(
    plan, halo_r, halo_l, own, tab_in, pst, hrd, mod, inv, dis, vel, load, mass,
    dis_out, vel_out, send,
    st, nd, rm, tab, win, grp, itn, turned,
):
    for c in range(COMP):
        if c < 15:
            mine = pst[c // 5, c % 5]
        elif c < 20:
            mine = hrd[c - 15]
        elif c < 25:
            mine = mod[c - 20]
        elif c == 25:
            mine = inv[...]
        else:
            mine = own[c - 26, LEFT : LEFT + OWN, :]
        at = c * ROWS
        scale, bias = 1.0, 0.0
        if C_H <= c < C_M:
            scale, bias = SLOPE, 1.0
        elif C_M <= c < C_Z:
            scale = TRIPLE
        st[at : at + LEFT, :] = halo_l[c * LEFT : (c + 1) * LEFT, :] * scale + bias
        st[at + LEFT : at + LEFT + OWN, :] = mine * scale + bias
        st[at + LEFT + OWN : at + BLOCKS, :] = halo_r[c * RIGHT : (c + 1) * RIGHT, :] * scale + bias
        st[at + BLOCKS : at + ROWS, :] = jnp.zeros((ROWS - BLOCKS, 128), F32)
    pinned = (lax.axis_index("span") == 0) & (lax.axis_index("grp") == 0)
    free_rows = jnp.where(
        pinned & (lax.broadcasted_iota(jnp.int32, (8, 128), 0) < 2), 0.0, 1.0
    ).astype(F32)
    for i in range(16):
        left = halo_l[COMP * LEFT + 6 * i : COMP * LEFT + 6 * i + 6, :]
        right = halo_r[COMP * RIGHT + 6 * i : COMP * RIGHT + 6 * i + 6, :]
        if i < 15:
            mine = (dis, vel, load)[i // 5][i % 5]
            if 5 <= i < 10:
                mine = mine * free_rows
            nd[i, 0:6, :] = left
            nd[i, 6:14, :] = mine
            nd[i, 14:20, :] = right
            nd[i, 20:32, :] = jnp.zeros((12, 128), F32)
        else:
            rm[0:6, :] = left
            rm[6:14, :] = mass[...]
            rm[14:20, :] = right
            rm[20:24, :] = jnp.zeros((4, 128), F32)
    weight = rm[...]
    there = weight > 0.0
    weight = jnp.where(there, STEP_TIME / jnp.where(there, weight, 1.0), 0.0)
    rm[...] = weight
    rm[6:14, :] = rm[6:14, :] * free_rows
    grp[...] = jnp.zeros(grp.shape, F32)

    member = lax.axis_index("grp")
    for outside, count, at, to in (
        (member == 0, LEFT, 0, 0),
        (member == lax.axis_size("grp") - 1, RIGHT, LEFT + OWN, LEFT),
    ):

        @pl.when(jnp.logical_not(outside))
        def _(count=count, at=at, to=to):
            def move(b, _):
                tab[to + b] = tab_in[at + b]
                return 0

            lax.fori_loop(0, count, move, 0)

        @pl.when(outside)
        def _(count=count, at=at, to=to):
            for o in range(0, count, 8):

                def put(j, row, side, values, o=o):
                    tab[to + o + j, row : row + 128, side] = values

                rows = [st[(C_I + k) * ROWS + at + o : (C_I + k) * ROWS + at + o + 8, :] for k in range(4)]
                table_octet(rows, turned, put, min(8, count - o))

    def table(b):
        if b < LEFT:
            return tab[b]
        return tab_in[b] if b < LEFT + OWN else tab[b - OWN]

    lane = lax.broadcasted_iota(jnp.int32, (NPAD, 128), 1)

    half_lane = lax.broadcasted_iota(jnp.int32, (8, 128), 1) < 64

    def comp(c, o):
        return st[c * ROWS + 8 * o : c * ROWS + 8 * o + 8, :]

    def update(o):
        at = 8 * o
        index = [comp(C_I + k, o).astype(jnp.int32) for k in range(4)]
        near = [i < 128 for i in index]
        place = [i & 127 for i in index]
        disp = []
        for d in range(5):
            low = win[d, at : at + 8, :]
            high = win[d, at + 2 : at + 10, :]
            disp.append([jnp.where(near[k], lanes(low, place[k]), lanes(high, place[k])) for k in range(4)])
        state = [([comp(i * 5 + p, o) for i in range(3)], comp(C_H + p, o), comp(C_M + p, o)) for p in range(5)]
        new_state, parts = element_octet(disp, state, comp(C_C, o), comp(C_Z, o))
        for p in range(5):
            plastic, level = new_state[p]
            for i in range(3):
                st[(i * 5 + p) * ROWS + at : (i * 5 + p) * ROWS + at + 8, :] = plastic[i]
            st[(C_H + p) * ROWS + at : (C_H + p) * ROWS + at + 8, :] = level
        for s in range(3):
            for d in range(5):
                if parts[s][d] is not None:
                    grp[o, s, pl.ds(d, 8, stride=8), :] = parts[s][d]

    def assemble(o, totals, first, last):
        for j in range(8):
            b = 8 * o + j
            if not first <= b < last:
                continue
            values = jnp.concatenate([grp[o, s, 8 * j : 8 * j + 8, :] for s in range(3)], axis=1)
            high = values.astype(BF16)
            low = (values - high.astype(F32)).astype(BF16)
            both = jnp.concatenate([high, low], axis=0)
            out = lax.dot_general(both, table(b), (((1,), (0,)), ((), ())), preferred_element_type=F32)
            out = out[0:8] + out[8:16]
            for h in range(2):
                piece = out[:, 128 * h : 128 * h + 128]
                place = (j % 2, b // 2 + h)
                totals[place] = piece if place not in totals else totals[place] + piece

    itn[...] = jnp.zeros(itn.shape, F32)
    for t in range(STEPS):
        reach_l, reach_r = 3 * (STEPS - t), 3 * (STEPS - t - 1)
        first, last = LEFT - reach_l, LEFT + OWN + reach_r
        for d in range(5):
            here = nd[d, 0:NPAD, :]
            rolled = pltpu.roll(here, 64, 1)
            after = pltpu.roll(nd[d, 1 : NPAD + 1, :], 64, 1)
            win[d, pl.ds(0, NPAD, stride=2), :] = here
            win[d, pl.ds(1, NPAD, stride=2), :] = jnp.where(lane < 64, rolled, after)
        totals = {}
        for o in range(first // 8, (last + 7) // 8):
            update(o)
            assemble(o, totals, first, last)
        zero = jnp.zeros((8, 128), F32)
        before = zero
        for r in range(NROW):
            odd = pltpu.roll(totals[1, r], 64, 1) if (1, r) in totals else zero
            itn[pl.ds(r, 8, stride=NPAD), :] = totals.get((0, r), zero) + jnp.where(half_lane, before, odd)
            before = odd
        weight = rm[...]
        for d in range(5):
            speed = nd[5 + d, 0:NPAD, :] + weight * (nd[10 + d, 0:NPAD, :] - itn[d * NPAD : (d + 1) * NPAD, :])
            nd[5 + d, 0:NPAD, :] = speed
            nd[d, 0:NPAD, :] = nd[d, 0:NPAD, :] + STEP_TIME * speed

    for d in range(5):
        dis_out[d] = nd[d, 6:14, :]
        vel_out[d] = nd[5 + d, 6:14, :]
    send[...] = jnp.zeros(send.shape, F32)
    for p in range(5):
        rows = slice((C_H + p) * ROWS + LEFT, (C_H + p) * ROWS + LEFT + OWN)
        st[rows, :] = (st[rows, :] - 1.0) * (1.0 / SLOPE)
    first = lax.axis_index("grp") * OWN
    for j in range(OWN):
        for q in range(5):
            send[plan[first + j], q] = st[pl.ds(4 * q * ROWS + LEFT + j, 4, stride=ROWS), :]


def unpack_kernel(recv, pst, hrd):
    for g in range(32):
        for q in range(5):
            values = recv[g, q]
            if q < 3:
                pst[pl.ds(128 * q + g, 4, stride=32), :] = values
            elif q == 3:
                pst[pl.ds(384 + g, 3, stride=32), :] = values[0:3]
                hrd[pl.ds(g, 1), :] = values[3:4]
            else:
                hrd[pl.ds(32 + g, 4, stride=32), :] = values


def vmem(count):
    return [pl.BlockSpec(memory_space=pltpu.VMEM) for _ in range(count)]


def on_device(
    displacement,
    velocity,
    nodal_load,
    nodal_mass,
    plastic_strain,
    hardening,
    ply_modulus,
    inverse_size,
    cost_map,
    migration_plan,
    block_nodes,
    corner_slot,
):
    dis = displacement.reshape(5, 8, 128)
    vel = velocity.reshape(5, 8, 128)
    load = nodal_load.reshape(5, 8, 128)
    mass = nodal_mass.reshape(8, 128)
    pst = jnp.transpose(plastic_strain[0], (1, 2, 0, 3))
    hrd = jnp.transpose(hardening[0], (1, 0, 2))
    mod = jnp.transpose(ply_modulus[0], (1, 0, 2))
    inv = inverse_size[0]
    smem = pl.BlockSpec(memory_space=pltpu.SMEM)
    hbm = pl.BlockSpec(memory_space=pltpu.HBM)
    to_right, to_left, own = pl.pallas_call(
        pack_kernel,
        out_shape=(
            jax.ShapeDtypeStruct((PL_ROWS, 128), F32),
            jax.ShapeDtypeStruct((PR_ROWS, 128), F32),
            jax.ShapeDtypeStruct((5, ROWS, 128), F32),
        ),
        in_specs=[hbm] * 11,
        out_specs=tuple(vmem(3)),
        scratch_shapes=[
            pltpu.VMEM((3, OWN, 256), jnp.int32),
            pltpu.VMEM((3, OWN, 4, 128), jnp.int32),
            pltpu.VMEM((3, 5, OWN, 128), F32),
            pltpu.VMEM((5, OWN, 128), F32),
            pltpu.VMEM((5, OWN, 128), F32),
            pltpu.VMEM((OWN, 128), F32),
            pltpu.VMEM((5, 8, 128), F32),
            pltpu.VMEM((5, 8, 128), F32),
            pltpu.VMEM((5, 8, 128), F32),
            pltpu.VMEM((8, 128), F32),
            pltpu.SMEM((512,), jnp.int32),
            pltpu.SemaphoreType.DMA((15,)),
        ],
        compiler_params=pltpu.CompilerParams(vmem_limit_bytes=8 << 20),
        name="pack",
    )(
        *[pltpu.with_memory_space_constraint(a, pltpu.HBM)
          for a in (cost_map[0], block_nodes[0], corner_slot[0], pst, hrd, mod, inv, dis, vel, load, mass)],
    )
    tables = pl.pallas_call(
        table_kernel,
        out_shape=jax.ShapeDtypeStruct((BLOCKS, 384, 256), BF16),
        in_specs=vmem(1),
        out_specs=vmem(1)[0],
        scratch_shapes=[pltpu.VMEM((128, 128), F32)],
        compiler_params=pltpu.CompilerParams(vmem_limit_bytes=8 << 20),
        cost_estimate=pl.CostEstimate(flops=40_000_000, bytes_accessed=12_000_000, transcendentals=0),
        name="tables",
    )(own)
    halo_r = shift(to_left, -1)
    halo_l = shift(to_right, 1)
    dis_out, vel_out, send = pl.pallas_call(
        step_kernel,
        out_shape=(
            jax.ShapeDtypeStruct((5, 8, 128), F32),
            jax.ShapeDtypeStruct((5, 8, 128), F32),
            jax.ShapeDtypeStruct((32, 5, 4, 128), F32),
        ),
        in_specs=[smem] + vmem(12),
        out_specs=tuple(vmem(3)),
        scratch_shapes=[
            pltpu.VMEM((COMP * ROWS + 8, 128), F32),
            pltpu.VMEM((15, 32, 128), F32),
            pltpu.VMEM((NPAD, 128), F32),
            pltpu.VMEM((LEFT + RIGHT, 384, 256), BF16),
            pltpu.VMEM((5, 56, 128), F32),
            pltpu.VMEM((ROWS // 8, 3, 64, 128), F32),
            pltpu.VMEM((8 * NPAD, 128), F32),
            pltpu.VMEM((128, 128), F32),
        ],
        compiler_params=pltpu.CompilerParams(vmem_limit_bytes=24 << 20),
        name="steps",
    )(migration_plan[0, :, 0], halo_r, halo_l, own, tables, pst, hrd, mod, inv, dis, vel, load, mass)
    recv = lax.all_to_all(send, "grp", split_axis=0, concat_axis=0, tiled=True)
    res_p, res_h = pl.pallas_call(
        unpack_kernel,
        out_shape=(
            jax.ShapeDtypeStruct((480, 128), F32),
            jax.ShapeDtypeStruct((160, 128), F32),
        ),
        in_specs=vmem(1),
        out_specs=tuple(vmem(2)),
        compiler_params=pltpu.CompilerParams(vmem_limit_bytes=4 << 20),
        name="unpack",
    )(recv)
    return (
        dis_out.reshape(1, 5, 1024),
        vel_out.reshape(1, 5, 1024),
        jnp.transpose(res_p.reshape(3, 5, 32, 128), (2, 0, 1, 3))[None],
        jnp.transpose(res_h.reshape(5, 32, 128), (1, 0, 2))[None],
    )


def solution(mesh):
    return jax.shard_map(
        on_device,
        mesh=mesh,
        in_specs=(
            P("span", None, "grp"),
            P("span", None, "grp"),
            P("span", None, "grp"),
            P("span", "grp"),
            P("span", "grp", None, None, None),
            P("span", "grp", None, None),
            P("span", "grp", None, None),
            P("span", "grp", None),
            P("span", None),
            P("span", None, None),
            P("span", None, None),
            P("span", None, None, None),
        ),
        out_specs=(
            P("span", None, "grp"),
            P("span", None, "grp"),
            P("span", "grp", None, None, None),
            P("span", "grp", None, None),
        ),
        check_vma=False,
    )
```

```python
import math

import jax
import jax.numpy as jnp
from jax import lax
from jax.experimental import pallas as pl
from jax.experimental.pallas import tpu as pltpu
from jax.sharding import PartitionSpec as P

NEWTON = 4
STEPS = 4
POISSON = 0.3
YIELD = 0.1
SATURATE = 0.1
RATE = 20.0
STEP_TIME = 0.25
THROUGH = (1.0 / 12, 4.0 / 12, 2.0 / 12, 4.0 / 12, 1.0 / 12)

OWN = 16
LEFT = 12
RIGHT = 9
BLOCKS = LEFT + OWN + RIGHT
ROWS = 40
NROW = 20
NPAD = 24
COMP = 31
PL_ROWS = 464
PR_ROWS = 368
C_H, C_M, C_Z, C_I, C_C = 15, 20, 25, 26, 30
F32 = jnp.float32
BF16 = jnp.bfloat16


def shift(shard, by):
    size = lax.axis_size(("span", "grp"))
    pairs = [(i, i + by) for i in range(size) if 0 <= i + by < size]
    return lax.ppermute(shard, ("span", "grp"), pairs)


def lanes(values, index):
    return jnp.take_along_axis(values, index, axis=1)


def nodal_rows(i):
    return (6 * i, 6) if i < 5 else (30 + 5 * (i - 5), 5)


def corner_spots(nodes, slots, base, put):
    for o in range(2):
        rows = slice(8 * o, 8 * o + 8)
        low, high = nodes[rows, 0:128], nodes[rows, 128:256]
        start = (base + 8 * o + lax.broadcasted_iota(jnp.int32, (8, 128), 0)) * 64
        for k in range(4):
            slot = slots[rows, k, :]
            lane = slot & 127
            node = jnp.where(slot < 128, lanes(low, lane), lanes(high, lane))
            put(k, o, (node - start).astype(F32))


def pack_kernel(
    cost_all, nodes_all, slots_all, pst_all, hrd_all, mod_all, inv_all, dis_all, vel_all, load_all, mass_all,
    to_right, to_left, own,
    nodes, slots, pst, hrd, mod, inv, dis, vel, load, mass, cost, sems,
):
    first = pl.multiple_of(lax.axis_index("grp") * OWN, OWN)
    total = nodes_all.shape[0]
    starts = (first, jnp.maximum(first - OWN, 0), jnp.minimum(first + OWN, total - OWN))
    lists = []
    for i, start in enumerate(starts):
        rows = pl.ds(pl.multiple_of(start, OWN), OWN)
        lists.append(pltpu.make_async_copy(nodes_all.at[rows], nodes.at[i], sems.at[8 + 2 * i]))
        lists.append(pltpu.make_async_copy(slots_all.at[rows], slots.at[i], sems.at[9 + 2 * i]))
    pairs = (
        (pst_all, pst), (hrd_all, hrd), (mod_all, mod), (inv_all, inv),
        (dis_all, dis), (vel_all, vel), (load_all, load), (mass_all, mass),
    )
    others = [pltpu.make_async_copy(source, target, sems.at[i]) for i, (source, target) in enumerate(pairs)]
    fetch_cost = pltpu.make_async_copy(cost_all, cost, sems.at[14])
    for copy in lists + others + [fetch_cost]:
        copy.start()
    for copy in lists:
        copy.wait()

    def put_own(k, o, values):
        own[k, LEFT + 8 * o : LEFT + 8 * o + 8, :] = values

    def put_left(k, o, values):
        if o == 0:
            own[k, 0:4, :] = values[4:8]
        else:
            own[k, 4:12, :] = values

    def put_right(k, o, values):
        if o == 0:
            own[k, LEFT + OWN : LEFT + OWN + 8, :] = values
        else:
            own[k, LEFT + OWN + 8 : BLOCKS, :] = values[0:1]

    corner_spots(nodes.at[0], slots.at[0], first, put_own)
    corner_spots(nodes.at[1], slots.at[1], first - OWN, put_left)
    corner_spots(nodes.at[2], slots.at[2], first + OWN, put_right)
    for k in range(4):
        own[k, BLOCKS:ROWS, :] = jnp.zeros((ROWS - BLOCKS, 128), F32)
    fetch_cost.wait()
    for j in range(OWN):
        own[4, LEFT + j : LEFT + j + 1, :] = jnp.full((1, 128), cost[first + j], jnp.int32).astype(F32)
    for copy in others:
        copy.wait()

    def rows_of(c, at, count):
        if c < 15:
            return pst[c // 5, c % 5, at : at + count, :]
        if c < 20:
            return hrd[c - 15, at : at + count, :]
        if c < 25:
            return mod[c - 20, at : at + count, :]
        if c == 25:
            return inv[at : at + count, :]
        return own[c - 26, LEFT + at : LEFT + at + count, :]

    for c in range(COMP):
        to_right[c * LEFT : (c + 1) * LEFT, :] = rows_of(c, OWN - LEFT, LEFT)
        to_left[c * RIGHT : (c + 1) * RIGHT, :] = rows_of(c, 0, RIGHT)
    for i in range(16):
        source = (dis, vel, load)[i // 5] if i < 15 else mass
        values = source[i % 5] if i < 15 else source[...]
        at, count = nodal_rows(i)
        to_right[COMP * LEFT + at : COMP * LEFT + at + count, :] = values[8 - count : 8]
        to_left[COMP * RIGHT + at : COMP * RIGHT + at + count, :] = values[0:count]


SLOPE = -RATE * math.log2(math.e)
DIAG = 1.0 - POISSON + POISSON * POISSON
CROSS = (4.0 * POISSON - 1.0 - POISSON * POISSON) / DIAG
SHEAR = 3.0 * (0.5 * (1.0 - POISSON)) ** 2 / DIAG
ELASTIC = 1.0 / (1.0 - POISSON * POISSON)
TRIPLE = 1.5 / (1.0 + POISSON)


def element_octet(disp, state, costs, inv):
    half = 0.5 * inv
    lean = [u[1] - u[3] for u in disp]
    rise = [u[2] - u[0] for u in disp]
    dx = [half * (s + t) for s, t in zip(lean, rise)]
    dy = [half * (t - s) for s, t in zip(lean, rise)]
    mean_a = 0.25 * ((disp[3][0] + disp[3][1]) + (disp[3][2] + disp[3][3]))
    mean_b = 0.25 * ((disp[4][0] + disp[4][1]) + (disp[4][2] + disp[4][3]))
    membrane = (dx[0], dy[1], dy[0] + dx[1])
    bending = (dx[3], dy[4], dy[3] + dx[4])
    shear = (dx[2] + mean_a, dy[2] + mean_b)
    far = [0.5 * b for b in bending]
    near = [0.25 * b for b in bending]
    fibre = (
        [m - b for m, b in zip(membrane, far)],
        [m - b for m, b in zip(membrane, near)],
        membrane,
        [m + b for m, b in zip(membrane, near)],
        [m + b for m, b in zip(membrane, far)],
    )
    active = [costs > float(t) for t in range(NEWTON)]
    offset = 0.5 * SATURATE * SLOPE
    new_state = []
    load = []
    g3_sum = None
    for p in range(5):
        plastic, level, g3 = state[p]
        e0, e1, e2 = [fibre[p][i] - plastic[i] for i in range(3)]
        square = e1 * (e1 + CROSS * e0) + e0 * e0 + SHEAR * (e2 * e2)
        norm = square * lax.rsqrt(jnp.maximum(square, 1e-37))
        q = (g3 * norm) * (SLOPE * ELASTIC / TRIPLE * math.sqrt(DIAG))
        base = q - SLOPE * (YIELD + SATURATE)
        decay = jnp.exp2(level)
        top = base + offset * decay
        flows = top < 0.0
        step = top / (g3 + decay)
        for turn in range(1, NEWTON):
            decay = jnp.exp2(level + step)
            moved = (base + decay * (step + offset)) / (g3 + decay)
            step = jnp.where(active[turn], moved, step)
        step = jnp.where(flows, step, 0.0)
        loss = (g3 * step) / jnp.minimum(q, SLOPE * YIELD)
        new_state.append(([plastic[0] + loss * e0, plastic[1] + loss * e1, plastic[2] + loss * e2], level + step))
        scale = (g3 * (THROUGH[p] * ELASTIC / TRIPLE)) * (1.0 - loss)
        load.append([scale * e0, scale * e1, scale * e2])
        part = THROUGH[p] * g3
        g3_sum = part if g3_sum is None else g3_sum + part
    force = [((load[0][i] + load[4][i]) + (load[1][i] + load[3][i])) + load[2][i] for i in range(3)]
    moment = [0.5 * (load[4][i] - load[0][i]) + 0.25 * (load[3][i] - load[1][i]) for i in range(3)]

    def resultant(s):
        a, b, c = half * s[0], half * s[1], half * s[2]
        return a + POISSON * b, POISSON * a + b, (0.5 * (1.0 - POISSON)) * c

    shear_modulus = g3_sum * (5.0 / 6.0 / (2.0 * (1.0 + POISSON)) / TRIPLE)
    q0, q1 = shear_modulus * shear[0], shear_modulus * shear[1]
    n0, n1, n2 = resultant(force)
    m0, m1, m2 = resultant(moment)
    k0, k1 = half * q0, half * q1
    lean_part = (n0 - n2, n2 - n1, k0 - k1, m0 - m2, m2 - m1)
    rise_part = (n0 + n2, n2 + n1, k0 + k1, m0 + m2, m2 + m1)
    even = (None, None, None, 0.25 * q0, 0.25 * q1)
    return new_state, (lean_part, rise_part, even)


def table_octet(rows, turned, put, count=8):
    turned[...] = jnp.transpose(jnp.concatenate(rows + [jnp.zeros((96, 128), F32)], axis=0))
    one, zero = jnp.ones((), BF16), jnp.zeros((), BF16)
    near = lax.broadcasted_iota(jnp.int32, (128, 128), 1).astype(F32)
    spots = (near.astype(BF16), (near + 128.0).astype(BF16))
    for j in range(count):
        column = [
            jnp.broadcast_to(turned[:, 8 * k + j : 8 * k + j + 1], (128, 128)).astype(BF16) for k in range(4)
        ]
        for half in range(2):
            hit = [jnp.where(c == spots[half], one, zero) for c in column]
            side = slice(128 * half, 128 * half + 128)
            put(j, 0, side, hit[1] - hit[3])
            put(j, 128, side, hit[2] - hit[0])
            put(j, 256, side, (hit[1] + hit[3]) + (hit[0] + hit[2]))


def table_kernel(spots, tab, turned):
    def octet(o, _):
        at = pl.multiple_of(o * 8, 8)

        def put(j, row, side, values):
            tab[at + j, row : row + 128, side] = values

        table_octet([spots[k, pl.ds(at, 8), :] for k in range(4)], turned, put)
        return 0

    lax.fori_loop(0, BLOCKS // 8, octet, 0)
    rest = BLOCKS // 8 * 8

    def put_rest(j, row, side, values):
        tab[rest + j, row : row + 128, side] = values

    table_octet([spots[k, rest : rest + 8, :] for k in range(4)], turned, put_rest, BLOCKS - rest)


def step_kernel(
    plan, halo_r, halo_l, own, tab_in, pst, hrd, mod, inv, dis, vel, load, mass,
    dis_out, vel_out, send,
    st, nd, rm, tab, win, grp, itn, turned,
):
    for c in range(COMP):
        if c < 15:
            mine = pst[c // 5, c % 5]
        elif c < 20:
            mine = hrd[c - 15]
        elif c < 25:
            mine = mod[c - 20]
        elif c == 25:
            mine = inv[...]
        else:
            mine = own[c - 26, LEFT : LEFT + OWN, :]
        at = c * ROWS
        scale, bias = 1.0, 0.0
        if C_H <= c < C_M:
            scale, bias = SLOPE, 1.0
        elif C_M <= c < C_Z:
            scale = TRIPLE
        st[at : at + LEFT, :] = halo_l[c * LEFT : (c + 1) * LEFT, :] * scale + bias
        st[at + LEFT : at + LEFT + OWN, :] = mine * scale + bias
        st[at + LEFT + OWN : at + BLOCKS, :] = halo_r[c * RIGHT : (c + 1) * RIGHT, :] * scale + bias
        st[at + BLOCKS : at + ROWS, :] = jnp.zeros((ROWS - BLOCKS, 128), F32)
    pinned = (lax.axis_index("span") == 0) & (lax.axis_index("grp") == 0)
    free_rows = jnp.where(
        pinned & (lax.broadcasted_iota(jnp.int32, (8, 128), 0) < 2), 0.0, 1.0
    ).astype(F32)
    for i in range(16):
        at, count = nodal_rows(i)
        left = halo_l[COMP * LEFT + at : COMP * LEFT + at + count, :]
        right = halo_r[COMP * RIGHT + at : COMP * RIGHT + at + count, :]
        if i < 15:
            mine = (dis, vel, load)[i // 5][i % 5]
            if 5 <= i < 10:
                mine = mine * free_rows
            nd[i, 0:1, :] = jnp.zeros((1, 128), F32)
            nd[i, 6 - count : 6, :] = left
            nd[i, 6:14, :] = mine
            nd[i, 14 : 14 + count, :] = right
            nd[i, 14 + count : 32, :] = jnp.zeros((18 - count, 128), F32)
        else:
            rm[0:1, :] = jnp.zeros((1, 128), F32)
            rm[6 - count : 6, :] = left
            rm[6:14, :] = mass[...]
            rm[14 : 14 + count, :] = right
            rm[14 + count : 24, :] = jnp.zeros((10 - count, 128), F32)
    weight = rm[...]
    there = weight > 0.0
    weight = jnp.where(there, STEP_TIME / jnp.where(there, weight, 1.0), 0.0)
    rm[...] = weight
    rm[6:14, :] = rm[6:14, :] * free_rows
    grp[...] = jnp.zeros(grp.shape, F32)

    member = lax.axis_index("grp")
    for outside, count, at, to in (
        (member == 0, LEFT, 0, 0),
        (member == lax.axis_size("grp") - 1, RIGHT, LEFT + OWN, LEFT),
    ):

        @pl.when(jnp.logical_not(outside))
        def _(count=count, at=at, to=to):
            def move(b, _):
                tab[to + b] = tab_in[at + b]
                return 0

            lax.fori_loop(0, count, move, 0)

        @pl.when(outside)
        def _(count=count, at=at, to=to):
            for o in range(0, count, 8):

                def put(j, row, side, values, o=o):
                    tab[to + o + j, row : row + 128, side] = values

                rows = [st[(C_I + k) * ROWS + at + o : (C_I + k) * ROWS + at + o + 8, :] for k in range(4)]
                table_octet(rows, turned, put, min(8, count - o))

    def table(b):
        if b < LEFT:
            return tab[b]
        return tab_in[b] if b < LEFT + OWN else tab[b - OWN]

    lane = lax.broadcasted_iota(jnp.int32, (NPAD, 128), 1)

    half_lane = lax.broadcasted_iota(jnp.int32, (8, 128), 1) < 64

    def comp(c, o):
        return st[c * ROWS + 8 * o : c * ROWS + 8 * o + 8, :]

    def update(o):
        at = 8 * o
        index = [comp(C_I + k, o).astype(jnp.int32) for k in range(4)]
        near = [i < 128 for i in index]
        place = [i & 127 for i in index]
        disp = []
        for d in range(5):
            low = win[d, at : at + 8, :]
            high = win[d, at + 2 : at + 10, :]
            disp.append([jnp.where(near[k], lanes(low, place[k]), lanes(high, place[k])) for k in range(4)])
        state = [([comp(i * 5 + p, o) for i in range(3)], comp(C_H + p, o), comp(C_M + p, o)) for p in range(5)]
        new_state, parts = element_octet(disp, state, comp(C_C, o), comp(C_Z, o))
        for p in range(5):
            plastic, level = new_state[p]
            for i in range(3):
                st[(i * 5 + p) * ROWS + at : (i * 5 + p) * ROWS + at + 8, :] = plastic[i]
            st[(C_H + p) * ROWS + at : (C_H + p) * ROWS + at + 8, :] = level
        for s in range(3):
            for d in range(5):
                if parts[s][d] is not None:
                    grp[o, s, pl.ds(d, 8, stride=8), :] = parts[s][d]

    def assemble(o, totals, first, last):
        for j in range(8):
            b = 8 * o + j
            if not first <= b < last:
                continue
            values = jnp.concatenate([grp[o, s, 8 * j : 8 * j + 8, :] for s in range(3)], axis=1)
            high = values.astype(BF16)
            low = (values - high.astype(F32)).astype(BF16)
            both = jnp.concatenate([high, low], axis=0)
            out = lax.dot_general(both, table(b), (((1,), (0,)), ((), ())), preferred_element_type=F32)
            out = out[0:8] + out[8:16]
            for h in range(2):
                piece = out[:, 128 * h : 128 * h + 128]
                place = (j % 2, b // 2 + h)
                totals[place] = piece if place not in totals else totals[place] + piece

    itn[...] = jnp.zeros(itn.shape, F32)
    for t in range(STEPS):
        reach_l, reach_r = 3 * (STEPS - t), 3 * (STEPS - t - 1)
        first, last = LEFT - reach_l, LEFT + OWN + reach_r
        for d in range(5):
            here = nd[d, 0:NPAD, :]
            rolled = pltpu.roll(here, 64, 1)
            after = pltpu.roll(nd[d, 1 : NPAD + 1, :], 64, 1)
            win[d, pl.ds(0, NPAD, stride=2), :] = here
            win[d, pl.ds(1, NPAD, stride=2), :] = jnp.where(lane < 64, rolled, after)
        totals = {}
        for o in range(first // 8, (last + 7) // 8):
            update(o)
            assemble(o, totals, first, last)
        zero = jnp.zeros((8, 128), F32)
        before = zero
        for r in range(NROW):
            odd = pltpu.roll(totals[1, r], 64, 1) if (1, r) in totals else zero
            itn[pl.ds(r, 8, stride=NPAD), :] = totals.get((0, r), zero) + jnp.where(half_lane, before, odd)
            before = odd
        weight = rm[...]
        for d in range(5):
            speed = nd[5 + d, 0:NPAD, :] + weight * (nd[10 + d, 0:NPAD, :] - itn[d * NPAD : (d + 1) * NPAD, :])
            nd[5 + d, 0:NPAD, :] = speed
            nd[d, 0:NPAD, :] = nd[d, 0:NPAD, :] + STEP_TIME * speed

    for d in range(5):
        dis_out[d] = nd[d, 6:14, :]
        vel_out[d] = nd[5 + d, 6:14, :]
    send[...] = jnp.zeros(send.shape, F32)
    for p in range(5):
        rows = slice((C_H + p) * ROWS + LEFT, (C_H + p) * ROWS + LEFT + OWN)
        st[rows, :] = (st[rows, :] - 1.0) * (1.0 / SLOPE)
    first = lax.axis_index("grp") * OWN
    for j in range(OWN):
        for q in range(5):
            send[plan[first + j], q] = st[pl.ds(4 * q * ROWS + LEFT + j, 4, stride=ROWS), :]


def unpack_kernel(recv, pst, hrd):
    for g in range(32):
        for q in range(5):
            values = recv[g, q]
            if q < 3:
                pst[pl.ds(128 * q + g, 4, stride=32), :] = values
            elif q == 3:
                pst[pl.ds(384 + g, 3, stride=32), :] = values[0:3]
                hrd[pl.ds(g, 1), :] = values[3:4]
            else:
                hrd[pl.ds(32 + g, 4, stride=32), :] = values


def vmem(count):
    return [pl.BlockSpec(memory_space=pltpu.VMEM) for _ in range(count)]


def on_device(
    displacement,
    velocity,
    nodal_load,
    nodal_mass,
    plastic_strain,
    hardening,
    ply_modulus,
    inverse_size,
    cost_map,
    migration_plan,
    block_nodes,
    corner_slot,
):
    dis = displacement.reshape(5, 8, 128)
    vel = velocity.reshape(5, 8, 128)
    load = nodal_load.reshape(5, 8, 128)
    mass = nodal_mass.reshape(8, 128)
    pst = jnp.transpose(plastic_strain[0], (1, 2, 0, 3))
    hrd = jnp.transpose(hardening[0], (1, 0, 2))
    mod = jnp.transpose(ply_modulus[0], (1, 0, 2))
    inv = inverse_size[0]
    smem = pl.BlockSpec(memory_space=pltpu.SMEM)
    hbm = pl.BlockSpec(memory_space=pltpu.HBM)
    to_right, to_left, own = pl.pallas_call(
        pack_kernel,
        out_shape=(
            jax.ShapeDtypeStruct((PL_ROWS, 128), F32),
            jax.ShapeDtypeStruct((PR_ROWS, 128), F32),
            jax.ShapeDtypeStruct((5, ROWS, 128), F32),
        ),
        in_specs=[hbm] * 11,
        out_specs=tuple(vmem(3)),
        scratch_shapes=[
            pltpu.VMEM((3, OWN, 256), jnp.int32),
            pltpu.VMEM((3, OWN, 4, 128), jnp.int32),
            pltpu.VMEM((3, 5, OWN, 128), F32),
            pltpu.VMEM((5, OWN, 128), F32),
            pltpu.VMEM((5, OWN, 128), F32),
            pltpu.VMEM((OWN, 128), F32),
            pltpu.VMEM((5, 8, 128), F32),
            pltpu.VMEM((5, 8, 128), F32),
            pltpu.VMEM((5, 8, 128), F32),
            pltpu.VMEM((8, 128), F32),
            pltpu.SMEM((512,), jnp.int32),
            pltpu.SemaphoreType.DMA((15,)),
        ],
        compiler_params=pltpu.CompilerParams(vmem_limit_bytes=8 << 20),
        name="pack",
    )(
        *[pltpu.with_memory_space_constraint(a, pltpu.HBM)
          for a in (cost_map[0], block_nodes[0], corner_slot[0], pst, hrd, mod, inv, dis, vel, load, mass)],
    )
    tables = pl.pallas_call(
        table_kernel,
        out_shape=jax.ShapeDtypeStruct((BLOCKS, 384, 256), BF16),
        in_specs=vmem(1),
        out_specs=vmem(1)[0],
        scratch_shapes=[pltpu.VMEM((128, 128), F32)],
        compiler_params=pltpu.CompilerParams(vmem_limit_bytes=8 << 20),
        cost_estimate=pl.CostEstimate(flops=40_000_000, bytes_accessed=12_000_000, transcendentals=0),
        name="tables",
    )(own)
    halo_r = shift(to_left, -1)
    halo_l = shift(to_right, 1)
    dis_out, vel_out, send = pl.pallas_call(
        step_kernel,
        out_shape=(
            jax.ShapeDtypeStruct((5, 8, 128), F32),
            jax.ShapeDtypeStruct((5, 8, 128), F32),
            jax.ShapeDtypeStruct((32, 5, 4, 128), F32),
        ),
        in_specs=[smem] + vmem(12),
        out_specs=tuple(vmem(3)),
        scratch_shapes=[
            pltpu.VMEM((COMP * ROWS + 8, 128), F32),
            pltpu.VMEM((15, 32, 128), F32),
            pltpu.VMEM((NPAD, 128), F32),
            pltpu.VMEM((LEFT + RIGHT, 384, 256), BF16),
            pltpu.VMEM((5, 56, 128), F32),
            pltpu.VMEM((ROWS // 8, 3, 64, 128), F32),
            pltpu.VMEM((8 * NPAD, 128), F32),
            pltpu.VMEM((128, 128), F32),
        ],
        compiler_params=pltpu.CompilerParams(vmem_limit_bytes=24 << 20),
        name="steps",
    )(migration_plan[0, :, 0], halo_r, halo_l, own, tables, pst, hrd, mod, inv, dis, vel, load, mass)
    recv = lax.all_to_all(send, "grp", split_axis=0, concat_axis=0, tiled=True)
    res_p, res_h = pl.pallas_call(
        unpack_kernel,
        out_shape=(
            jax.ShapeDtypeStruct((480, 128), F32),
            jax.ShapeDtypeStruct((160, 128), F32),
        ),
        in_specs=vmem(1),
        out_specs=tuple(vmem(2)),
        compiler_params=pltpu.CompilerParams(vmem_limit_bytes=4 << 20),
        name="unpack",
    )(recv)
    return (
        dis_out.reshape(1, 5, 1024),
        vel_out.reshape(1, 5, 1024),
        jnp.transpose(res_p.reshape(3, 5, 32, 128), (2, 0, 1, 3))[None],
        jnp.transpose(res_h.reshape(5, 32, 128), (1, 0, 2))[None],
    )


def solution(mesh):
    return jax.shard_map(
        on_device,
        mesh=mesh,
        in_specs=(
            P("span", None, "grp"),
            P("span", None, "grp"),
            P("span", None, "grp"),
            P("span", "grp"),
            P("span", "grp", None, None, None),
            P("span", "grp", None, None),
            P("span", "grp", None, None),
            P("span", "grp", None),
            P("span", None),
            P("span", None, None),
            P("span", None, None),
            P("span", None, None, None),
        ),
        out_specs=(
            P("span", None, "grp"),
            P("span", None, "grp"),
            P("span", "grp", None, None, None),
            P("span", "grp", None, None),
        ),
        check_vma=False,
    )
```

```python
import math

import jax
import jax.numpy as jnp
from jax import lax
from jax.experimental import pallas as pl
from jax.experimental.pallas import tpu as pltpu
from jax.sharding import PartitionSpec as P

NEWTON = 4
STEPS = 4
POISSON = 0.3
YIELD = 0.1
SATURATE = 0.1
RATE = 20.0
STEP_TIME = 0.25
THROUGH = (1.0 / 12, 4.0 / 12, 2.0 / 12, 4.0 / 12, 1.0 / 12)

OWN = 16
LEFT = 12
RIGHT = 9
BLOCKS = LEFT + OWN + RIGHT
ROWS = 40
NROW = 20
NPAD = 24
COMP = 31
PL_ROWS = 464
PR_ROWS = 368
C_H, C_M, C_Z, C_I, C_C = 15, 20, 25, 26, 30
F32 = jnp.float32
BF16 = jnp.bfloat16


def shift(shard, by):
    size = lax.axis_size(("span", "grp"))
    pairs = [(i, i + by) for i in range(size) if 0 <= i + by < size]
    return lax.ppermute(shard, ("span", "grp"), pairs)


def lanes(values, index):
    return jnp.take_along_axis(values, index, axis=1)


def nodal_rows(i):
    return (6 * i, 6) if i < 5 else (30 + 5 * (i - 5), 5)


def corner_spots(nodes, slots, base, put):
    for o in range(2):
        rows = slice(8 * o, 8 * o + 8)
        low, high = nodes[rows, 0:128], nodes[rows, 128:256]
        start = (base + 8 * o + lax.broadcasted_iota(jnp.int32, (8, 128), 0)) * 64
        for k in range(4):
            slot = slots[rows, k, :]
            lane = slot & 127
            node = jnp.where(slot < 128, lanes(low, lane), lanes(high, lane))
            put(k, o, (node - start).astype(F32))


def pack_kernel(
    cost_all, nodes_all, slots_all, pst_all, hrd_all, mod_all, inv_all, dis_all, vel_all, load_all, mass_all,
    to_right, to_left, own,
    nodes, slots, pst, hrd, mod, inv, dis, vel, load, mass, cost, sems,
):
    first = pl.multiple_of(lax.axis_index("grp") * OWN, OWN)
    total = nodes_all.shape[0]
    starts = (first, jnp.maximum(first - OWN, 0), jnp.minimum(first + OWN, total - OWN))
    lists = []
    for i, start in enumerate(starts):
        rows = pl.ds(pl.multiple_of(start, OWN), OWN)
        lists.append(pltpu.make_async_copy(nodes_all.at[rows], nodes.at[i], sems.at[8 + 2 * i]))
        lists.append(pltpu.make_async_copy(slots_all.at[rows], slots.at[i], sems.at[9 + 2 * i]))
    pairs = (
        (pst_all, pst), (hrd_all, hrd), (mod_all, mod), (inv_all, inv),
        (dis_all, dis), (vel_all, vel), (load_all, load), (mass_all, mass),
    )
    others = [pltpu.make_async_copy(source, target, sems.at[i]) for i, (source, target) in enumerate(pairs)]
    fetch_cost = pltpu.make_async_copy(cost_all, cost, sems.at[14])
    for copy in lists + others + [fetch_cost]:
        copy.start()
    for copy in lists:
        copy.wait()

    def put_own(k, o, values):
        own[k, LEFT + 8 * o : LEFT + 8 * o + 8, :] = values

    def put_left(k, o, values):
        if o == 0:
            own[k, 0:4, :] = values[4:8]
        else:
            own[k, 4:12, :] = values

    def put_right(k, o, values):
        if o == 0:
            own[k, LEFT + OWN : LEFT + OWN + 8, :] = values
        else:
            own[k, LEFT + OWN + 8 : BLOCKS, :] = values[0:1]

    corner_spots(nodes.at[0], slots.at[0], first, put_own)
    corner_spots(nodes.at[1], slots.at[1], first - OWN, put_left)
    corner_spots(nodes.at[2], slots.at[2], first + OWN, put_right)
    for k in range(4):
        own[k, BLOCKS:ROWS, :] = jnp.zeros((ROWS - BLOCKS, 128), F32)
    fetch_cost.wait()
    for j in range(OWN):
        own[4, LEFT + j : LEFT + j + 1, :] = jnp.full((1, 128), cost[first + j], jnp.int32).astype(F32)
    for copy in others:
        copy.wait()

    def rows_of(c, at, count):
        if c < 15:
            return pst[c // 5, c % 5, at : at + count, :]
        if c < 20:
            return hrd[c - 15, at : at + count, :]
        if c < 25:
            return mod[c - 20, at : at + count, :]
        if c == 25:
            return inv[at : at + count, :]
        return own[c - 26, LEFT + at : LEFT + at + count, :]

    for c in range(COMP):
        to_right[c * LEFT : (c + 1) * LEFT, :] = rows_of(c, OWN - LEFT, LEFT)
        to_left[c * RIGHT : (c + 1) * RIGHT, :] = rows_of(c, 0, RIGHT)
    for i in range(16):
        source = (dis, vel, load)[i // 5] if i < 15 else mass
        values = source[i % 5] if i < 15 else source[...]
        at, count = nodal_rows(i)
        to_right[COMP * LEFT + at : COMP * LEFT + at + count, :] = values[8 - count : 8]
        to_left[COMP * RIGHT + at : COMP * RIGHT + at + count, :] = values[0:count]


SLOPE = -RATE * math.log2(math.e)
DIAG = 1.0 - POISSON + POISSON * POISSON
CROSS = (4.0 * POISSON - 1.0 - POISSON * POISSON) / DIAG
SHEAR = 3.0 * (0.5 * (1.0 - POISSON)) ** 2 / DIAG
ELASTIC = 1.0 / (1.0 - POISSON * POISSON)
TRIPLE = 1.5 / (1.0 + POISSON)


def element_octet(disp, state, costs, inv):
    half = 0.5 * inv
    lean = [u[1] - u[3] for u in disp]
    rise = [u[2] - u[0] for u in disp]
    dx = [half * (s + t) for s, t in zip(lean, rise)]
    dy = [half * (t - s) for s, t in zip(lean, rise)]
    mean_a = 0.25 * ((disp[3][0] + disp[3][1]) + (disp[3][2] + disp[3][3]))
    mean_b = 0.25 * ((disp[4][0] + disp[4][1]) + (disp[4][2] + disp[4][3]))
    membrane = (dx[0], dy[1], dy[0] + dx[1])
    bending = (dx[3], dy[4], dy[3] + dx[4])
    shear = (dx[2] + mean_a, dy[2] + mean_b)
    far = [0.5 * b for b in bending]
    near = [0.25 * b for b in bending]
    fibre = (
        [m - b for m, b in zip(membrane, far)],
        [m - b for m, b in zip(membrane, near)],
        membrane,
        [m + b for m, b in zip(membrane, near)],
        [m + b for m, b in zip(membrane, far)],
    )
    active = [costs > float(t) for t in range(NEWTON)]
    offset = 0.5 * SATURATE * SLOPE
    new_state = []
    load = []
    g3_sum = None
    for p in range(5):
        plastic, level, g3 = state[p]
        e0, e1, e2 = [fibre[p][i] - plastic[i] for i in range(3)]
        square = e1 * (e1 + CROSS * e0) + e0 * e0 + SHEAR * (e2 * e2)
        norm = square * lax.rsqrt(jnp.maximum(square, 1e-37))
        q = (g3 * norm) * (SLOPE * ELASTIC / TRIPLE * math.sqrt(DIAG))
        base = q - SLOPE * (YIELD + SATURATE)
        decay = jnp.exp2(level)
        top = base + offset * decay
        flows = top < 0.0
        step = top / (g3 + decay)
        for turn in range(1, NEWTON):
            decay = jnp.exp2(level + step)
            moved = (base + decay * (step + offset)) / (g3 + decay)
            step = jnp.where(active[turn], moved, step)
        step = jnp.where(flows, step, 0.0)
        loss = (g3 * step) / jnp.minimum(q, SLOPE * YIELD)
        new_state.append(([plastic[0] + loss * e0, plastic[1] + loss * e1, plastic[2] + loss * e2], level + step))
        scale = (g3 * (THROUGH[p] * ELASTIC / TRIPLE)) * (1.0 - loss)
        load.append([scale * e0, scale * e1, scale * e2])
        part = THROUGH[p] * g3
        g3_sum = part if g3_sum is None else g3_sum + part
    force = [((load[0][i] + load[4][i]) + (load[1][i] + load[3][i])) + load[2][i] for i in range(3)]
    moment = [0.5 * (load[4][i] - load[0][i]) + 0.25 * (load[3][i] - load[1][i]) for i in range(3)]

    def resultant(s):
        a, b, c = half * s[0], half * s[1], half * s[2]
        return a + POISSON * b, POISSON * a + b, (0.5 * (1.0 - POISSON)) * c

    shear_modulus = g3_sum * (5.0 / 6.0 / (2.0 * (1.0 + POISSON)) / TRIPLE)
    q0, q1 = shear_modulus * shear[0], shear_modulus * shear[1]
    n0, n1, n2 = resultant(force)
    m0, m1, m2 = resultant(moment)
    k0, k1 = half * q0, half * q1
    lean_part = (n0 - n2, n2 - n1, k0 - k1, m0 - m2, m2 - m1)
    rise_part = (n0 + n2, n2 + n1, k0 + k1, m0 + m2, m2 + m1)
    even = (None, None, None, 0.25 * q0, 0.25 * q1)
    return new_state, (lean_part, rise_part, even)


def table_octet(rows, turned, put, count=8):
    turned[...] = jnp.transpose(jnp.concatenate(rows + [jnp.zeros((96, 128), F32)], axis=0))
    one, zero = jnp.ones((), BF16), jnp.zeros((), BF16)
    near = lax.broadcasted_iota(jnp.int32, (128, 128), 1).astype(F32)
    spots = (near.astype(BF16), (near + 128.0).astype(BF16))
    for j in range(count):
        column = [
            jnp.broadcast_to(turned[:, 8 * k + j : 8 * k + j + 1], (128, 128)).astype(BF16) for k in range(4)
        ]
        for half in range(2):
            hit = [jnp.where(c == spots[half], one, zero) for c in column]
            side = slice(128 * half, 128 * half + 128)
            put(j, 0, side, hit[1] - hit[3])
            put(j, 128, side, hit[2] - hit[0])
            put(j, 256, side, (hit[1] + hit[3]) + (hit[0] + hit[2]))


def table_kernel(spots, tab, turned):
    def octet(o, _):
        at = pl.multiple_of(o * 8, 8)

        def put(j, row, side, values):
            tab[at + j, row : row + 128, side] = values

        table_octet([spots[k, pl.ds(at, 8), :] for k in range(4)], turned, put)
        return 0

    lax.fori_loop(0, BLOCKS // 8, octet, 0)
    rest = BLOCKS // 8 * 8

    def put_rest(j, row, side, values):
        tab[rest + j, row : row + 128, side] = values

    table_octet([spots[k, rest : rest + 8, :] for k in range(4)], turned, put_rest, BLOCKS - rest)


def step_kernel(
    plan, halo_r, halo_l, own, tab_in, pst, hrd, mod, inv, dis, vel, load, mass,
    dis_out, vel_out, send, tab,
    st, nd, rm, win, grp, itn, turned,
):
    for c in range(COMP):
        if c < 15:
            mine = pst[c // 5, c % 5]
        elif c < 20:
            mine = hrd[c - 15]
        elif c < 25:
            mine = mod[c - 20]
        elif c == 25:
            mine = inv[...]
        else:
            mine = own[c - 26, LEFT : LEFT + OWN, :]
        at = c * ROWS
        scale, bias = 1.0, 0.0
        if C_H <= c < C_M:
            scale, bias = SLOPE, 1.0
        elif C_M <= c < C_Z:
            scale = TRIPLE
        st[at : at + LEFT, :] = halo_l[c * LEFT : (c + 1) * LEFT, :] * scale + bias
        st[at + LEFT : at + LEFT + OWN, :] = mine * scale + bias
        st[at + LEFT + OWN : at + BLOCKS, :] = halo_r[c * RIGHT : (c + 1) * RIGHT, :] * scale + bias
        st[at + BLOCKS : at + ROWS, :] = jnp.zeros((ROWS - BLOCKS, 128), F32)
    pinned = (lax.axis_index("span") == 0) & (lax.axis_index("grp") == 0)
    free_rows = jnp.where(
        pinned & (lax.broadcasted_iota(jnp.int32, (8, 128), 0) < 2), 0.0, 1.0
    ).astype(F32)
    for i in range(16):
        at, count = nodal_rows(i)
        left = halo_l[COMP * LEFT + at : COMP * LEFT + at + count, :]
        right = halo_r[COMP * RIGHT + at : COMP * RIGHT + at + count, :]
        if i < 15:
            mine = (dis, vel, load)[i // 5][i % 5]
            if 5 <= i < 10:
                mine = mine * free_rows
            nd[i, 0:1, :] = jnp.zeros((1, 128), F32)
            nd[i, 6 - count : 6, :] = left
            nd[i, 6:14, :] = mine
            nd[i, 14 : 14 + count, :] = right
            nd[i, 14 + count : 32, :] = jnp.zeros((18 - count, 128), F32)
        else:
            rm[0:1, :] = jnp.zeros((1, 128), F32)
            rm[6 - count : 6, :] = left
            rm[6:14, :] = mass[...]
            rm[14 : 14 + count, :] = right
            rm[14 + count : 24, :] = jnp.zeros((10 - count, 128), F32)
    weight = rm[...]
    there = weight > 0.0
    weight = jnp.where(there, STEP_TIME / jnp.where(there, weight, 1.0), 0.0)
    rm[...] = weight
    rm[6:14, :] = rm[6:14, :] * free_rows
    grp[...] = jnp.zeros(grp.shape, F32)

    member = lax.axis_index("grp")
    for outside, count, at in (
        (member == 0, LEFT, 0),
        (member == lax.axis_size("grp") - 1, RIGHT, LEFT + OWN),
    ):

        @pl.when(outside)
        def _(count=count, at=at):
            for o in range(0, count, 8):

                def put(j, row, side, values, o=o):
                    tab[at + o + j, row : row + 128, side] = values

                rows = [st[(C_I + k) * ROWS + at + o : (C_I + k) * ROWS + at + o + 8, :] for k in range(4)]
                table_octet(rows, turned, put, min(8, count - o))

    lane = lax.broadcasted_iota(jnp.int32, (NPAD, 128), 1)

    half_lane = lax.broadcasted_iota(jnp.int32, (8, 128), 1) < 64

    def comp(c, o):
        return st[c * ROWS + 8 * o : c * ROWS + 8 * o + 8, :]

    def update(o):
        at = 8 * o
        index = [comp(C_I + k, o).astype(jnp.int32) for k in range(4)]
        near = [i < 128 for i in index]
        place = [i & 127 for i in index]
        disp = []
        for d in range(5):
            low = win[d, at : at + 8, :]
            high = win[d, at + 2 : at + 10, :]
            disp.append([jnp.where(near[k], lanes(low, place[k]), lanes(high, place[k])) for k in range(4)])
        state = [([comp(i * 5 + p, o) for i in range(3)], comp(C_H + p, o), comp(C_M + p, o)) for p in range(5)]
        new_state, parts = element_octet(disp, state, comp(C_C, o), comp(C_Z, o))
        for p in range(5):
            plastic, level = new_state[p]
            for i in range(3):
                st[(i * 5 + p) * ROWS + at : (i * 5 + p) * ROWS + at + 8, :] = plastic[i]
            st[(C_H + p) * ROWS + at : (C_H + p) * ROWS + at + 8, :] = level
        for s in range(3):
            for d in range(5):
                if parts[s][d] is not None:
                    grp[o, s, pl.ds(d, 8, stride=8), :] = parts[s][d]

    def assemble(o, totals, first, last):
        for j in range(8):
            b = 8 * o + j
            if not first <= b < last:
                continue
            values = jnp.concatenate([grp[o, s, 8 * j : 8 * j + 8, :] for s in range(3)], axis=1)
            high = values.astype(BF16)
            low = (values - high.astype(F32)).astype(BF16)
            both = jnp.concatenate([high, low], axis=0)
            out = lax.dot_general(both, tab[b], (((1,), (0,)), ((), ())), preferred_element_type=F32)
            out = out[0:8] + out[8:16]
            for h in range(2):
                piece = out[:, 128 * h : 128 * h + 128]
                place = (j % 2, b // 2 + h)
                totals[place] = piece if place not in totals else totals[place] + piece

    itn[...] = jnp.zeros(itn.shape, F32)
    for t in range(STEPS):
        reach_l, reach_r = 3 * (STEPS - t), 3 * (STEPS - t - 1)
        first, last = LEFT - reach_l, LEFT + OWN + reach_r
        for d in range(5):
            here = nd[d, 0:NPAD, :]
            rolled = pltpu.roll(here, 64, 1)
            after = pltpu.roll(nd[d, 1 : NPAD + 1, :], 64, 1)
            win[d, pl.ds(0, NPAD, stride=2), :] = here
            win[d, pl.ds(1, NPAD, stride=2), :] = jnp.where(lane < 64, rolled, after)
        totals = {}
        for o in range(first // 8, (last + 7) // 8):
            update(o)
            assemble(o, totals, first, last)
        zero = jnp.zeros((8, 128), F32)
        before = zero
        for r in range(NROW):
            odd = pltpu.roll(totals[1, r], 64, 1) if (1, r) in totals else zero
            itn[pl.ds(r, 8, stride=NPAD), :] = totals.get((0, r), zero) + jnp.where(half_lane, before, odd)
            before = odd
        weight = rm[...]
        for d in range(5):
            speed = nd[5 + d, 0:NPAD, :] + weight * (nd[10 + d, 0:NPAD, :] - itn[d * NPAD : (d + 1) * NPAD, :])
            nd[5 + d, 0:NPAD, :] = speed
            nd[d, 0:NPAD, :] = nd[d, 0:NPAD, :] + STEP_TIME * speed

    for d in range(5):
        dis_out[d] = nd[d, 6:14, :]
        vel_out[d] = nd[5 + d, 6:14, :]
    send[...] = jnp.zeros(send.shape, F32)
    for p in range(5):
        rows = slice((C_H + p) * ROWS + LEFT, (C_H + p) * ROWS + LEFT + OWN)
        st[rows, :] = (st[rows, :] - 1.0) * (1.0 / SLOPE)
    first = lax.axis_index("grp") * OWN
    for j in range(OWN):
        for q in range(5):
            send[plan[first + j], q] = st[pl.ds(4 * q * ROWS + LEFT + j, 4, stride=ROWS), :]


def unpack_kernel(recv, pst, hrd):
    for g in range(32):
        for q in range(5):
            values = recv[g, q]
            if q < 3:
                pst[pl.ds(128 * q + g, 4, stride=32), :] = values
            elif q == 3:
                pst[pl.ds(384 + g, 3, stride=32), :] = values[0:3]
                hrd[pl.ds(g, 1), :] = values[3:4]
            else:
                hrd[pl.ds(32 + g, 4, stride=32), :] = values


def vmem(count):
    return [pl.BlockSpec(memory_space=pltpu.VMEM) for _ in range(count)]


def on_device(
    displacement,
    velocity,
    nodal_load,
    nodal_mass,
    plastic_strain,
    hardening,
    ply_modulus,
    inverse_size,
    cost_map,
    migration_plan,
    block_nodes,
    corner_slot,
):
    dis = displacement.reshape(5, 8, 128)
    vel = velocity.reshape(5, 8, 128)
    load = nodal_load.reshape(5, 8, 128)
    mass = nodal_mass.reshape(8, 128)
    pst = jnp.transpose(plastic_strain[0], (1, 2, 0, 3))
    hrd = jnp.transpose(hardening[0], (1, 0, 2))
    mod = jnp.transpose(ply_modulus[0], (1, 0, 2))
    inv = inverse_size[0]
    smem = pl.BlockSpec(memory_space=pltpu.SMEM)
    hbm = pl.BlockSpec(memory_space=pltpu.HBM)
    to_right, to_left, own = pl.pallas_call(
        pack_kernel,
        out_shape=(
            jax.ShapeDtypeStruct((PL_ROWS, 128), F32),
            jax.ShapeDtypeStruct((PR_ROWS, 128), F32),
            jax.ShapeDtypeStruct((5, ROWS, 128), F32),
        ),
        in_specs=[hbm] * 11,
        out_specs=tuple(vmem(3)),
        scratch_shapes=[
            pltpu.VMEM((3, OWN, 256), jnp.int32),
            pltpu.VMEM((3, OWN, 4, 128), jnp.int32),
            pltpu.VMEM((3, 5, OWN, 128), F32),
            pltpu.VMEM((5, OWN, 128), F32),
            pltpu.VMEM((5, OWN, 128), F32),
            pltpu.VMEM((OWN, 128), F32),
            pltpu.VMEM((5, 8, 128), F32),
            pltpu.VMEM((5, 8, 128), F32),
            pltpu.VMEM((5, 8, 128), F32),
            pltpu.VMEM((8, 128), F32),
            pltpu.SMEM((512,), jnp.int32),
            pltpu.SemaphoreType.DMA((15,)),
        ],
        compiler_params=pltpu.CompilerParams(vmem_limit_bytes=8 << 20),
        name="pack",
    )(
        *[pltpu.with_memory_space_constraint(a, pltpu.HBM)
          for a in (cost_map[0], block_nodes[0], corner_slot[0], pst, hrd, mod, inv, dis, vel, load, mass)],
    )
    tables = pl.pallas_call(
        table_kernel,
        out_shape=jax.ShapeDtypeStruct((BLOCKS, 384, 256), BF16),
        in_specs=vmem(1),
        out_specs=vmem(1)[0],
        scratch_shapes=[pltpu.VMEM((128, 128), F32)],
        compiler_params=pltpu.CompilerParams(vmem_limit_bytes=8 << 20),
        cost_estimate=pl.CostEstimate(flops=40_000_000, bytes_accessed=12_000_000, transcendentals=0),
        name="tables",
    )(own)
    halo_r = shift(to_left, -1)
    halo_l = shift(to_right, 1)
    dis_out, vel_out, send, _ = pl.pallas_call(
        step_kernel,
        out_shape=(
            jax.ShapeDtypeStruct((5, 8, 128), F32),
            jax.ShapeDtypeStruct((5, 8, 128), F32),
            jax.ShapeDtypeStruct((32, 5, 4, 128), F32),
            jax.ShapeDtypeStruct((BLOCKS, 384, 256), BF16),
        ),
        in_specs=[smem] + vmem(12),
        out_specs=tuple(vmem(4)),
        input_output_aliases={4: 3},
        scratch_shapes=[
            pltpu.VMEM((COMP * ROWS + 8, 128), F32),
            pltpu.VMEM((15, 32, 128), F32),
            pltpu.VMEM((NPAD, 128), F32),
            pltpu.VMEM((5, 56, 128), F32),
            pltpu.VMEM((ROWS // 8, 3, 64, 128), F32),
            pltpu.VMEM((8 * NPAD, 128), F32),
            pltpu.VMEM((128, 128), F32),
        ],
        compiler_params=pltpu.CompilerParams(vmem_limit_bytes=24 << 20),
        name="steps",
    )(migration_plan[0, :, 0], halo_r, halo_l, own, tables, pst, hrd, mod, inv, dis, vel, load, mass)
    recv = lax.all_to_all(send, "grp", split_axis=0, concat_axis=0, tiled=True)
    res_p, res_h = pl.pallas_call(
        unpack_kernel,
        out_shape=(
            jax.ShapeDtypeStruct((480, 128), F32),
            jax.ShapeDtypeStruct((160, 128), F32),
        ),
        in_specs=vmem(1),
        out_specs=tuple(vmem(2)),
        compiler_params=pltpu.CompilerParams(vmem_limit_bytes=4 << 20),
        name="unpack",
    )(recv)
    return (
        dis_out.reshape(1, 5, 1024),
        vel_out.reshape(1, 5, 1024),
        jnp.transpose(res_p.reshape(3, 5, 32, 128), (2, 0, 1, 3))[None],
        jnp.transpose(res_h.reshape(5, 32, 128), (1, 0, 2))[None],
    )


def solution(mesh):
    return jax.shard_map(
        on_device,
        mesh=mesh,
        in_specs=(
            P("span", None, "grp"),
            P("span", None, "grp"),
            P("span", None, "grp"),
            P("span", "grp"),
            P("span", "grp", None, None, None),
            P("span", "grp", None, None),
            P("span", "grp", None, None),
            P("span", "grp", None),
            P("span", None),
            P("span", None, None),
            P("span", None, None),
            P("span", None, None, None),
        ),
        out_specs=(
            P("span", None, "grp"),
            P("span", None, "grp"),
            P("span", "grp", None, None, None),
            P("span", "grp", None, None),
        ),
        check_vma=False,
    )
```
